32 devices in a mesh: parts: 2 (over x), seq: 8 (over z, y), dp: 2 (over core).
Axes of the slice: x: 2, y: 2, z: 4, core: 2. Of those that a mesh axis runs over, the one named last changes fastest.
Arguments:
- activations: bfloat16 [8, 2048, 1024], P(('parts', 'dp'), 'seq'), parts along dimension 0, may hold values from -36 to 36, as said below
- cotangent: bfloat16 [8, 2048, 1024], P(('parts', 'dp'), 'seq'), parts along dimension 0, may hold values from -6 to 6
- conv_one: bfloat16 [1024, 3, 512], P(('seq', 'dp')), may hold values from -0.109375 to 0.109375
- mix_one: bfloat16 [512, 1024], P(('seq', 'dp')), may hold values from -0.25 to 0.25
- conv_two: bfloat16 [1024, 3, 512], P(('seq', 'dp')), may hold values from -0.109375 to 0.109375
- mix_two: bfloat16 [512, 1024], P(('seq', 'dp')), may hold values from -0.25 to 0.25
Outputs:
- input_grad: bfloat16 [8, 2048, 1024], P(('parts', 'dp'), 'seq'), parts along dimension 0
- grad_conv_one: float32 [2048, 3, 512], P(('parts', 'seq', 'dp')), parts along dimension 0
- grad_mix_one: float32 [1024, 1024], P(('parts', 'seq', 'dp')), parts along dimension 0
- grad_conv_two: float32 [2048, 3, 512], P(('parts', 'seq', 'dp')), parts along dimension 0
- grad_mix_two: float32 [1024, 1024], P(('parts', 'seq', 'dp')), parts along dimension 0
The draws below stay inside these ranges and needn't reach their ends.
There are 2 independent parts, one for each index of `parts`. The reference program is written for one: setup_inputs(seed, part) draws one part's arguments, and reference() takes and returns one part's arrays. A program takes and returns all parts, laid end to end along the dimension named above; an argument that names none is the same for every part. Nothing has to cross between parts.
Inputs may be any that keep to these rules, and one draw needn't show every extreme that they name: activations of earlier layers.
All inputs are finite; a program needn't handle non-finite values.
Results may differ from the reference program's by a relative error of at most 0.007.
Values may be sent and summed in bfloat16 or wider, within the bound.
No kernel may reach another device: no remote copies, remote signals or barrier semaphores. Data moves between devices by JAX's collectives and lax.ppermute only.
A program may use at most 128 MiB of HBM per device.

```python
import math
import jax
import jax.numpy as jnp
from jax import lax

CHANNELS = 1024
MIDDLE = 512
DILATE_ONE = 64
DILATE_TWO = 128
WINDOW_BINS = 2048
WINDOWS = 4


def draw_activations(key, part):
    first, second, third = jax.random.split(key, 3)
    shape = (WINDOWS, WINDOW_BINS, CHANNELS)
    base = jax.random.truncated_normal(first, -4.0, 4.0, shape, jnp.float32)
    channel_scale = jnp.exp(jax.random.uniform(second, (CHANNELS,), jnp.float32, math.log(0.3), math.log(3.0)))
    row_scale = jnp.exp(jax.random.uniform(third, (WINDOWS, WINDOW_BINS, 1), jnp.float32, math.log(0.3), math.log(3.0)))
    return (base * channel_scale * row_scale).astype(jnp.bfloat16)


def level_of(own_key, dims, pieces, low, high):
    factor_of = 1.0
    for axis_at, shards_of in pieces:
        steps = jax.random.uniform(jax.random.fold_in(jax.random.fold_in(own_key, 6), axis_at), (shards_of,), jnp.float32, low / len(pieces), high / len(pieces))
        factor_of = factor_of * jnp.repeat(jnp.exp(steps), dims[axis_at] // shards_of).reshape((-1,) + (1,) * (len(dims) - 1 - axis_at))
    return factor_of


def normal_values(stream_key, shape, deviation, reach, pieces=(), dtype=jnp.bfloat16):
    entries = jax.random.normal(stream_key, shape, jnp.float32) * deviation
    if len(pieces) > 0:
        entries = level_of(stream_key, shape, pieces, -0.22, 0.18) * entries
    return jnp.clip(entries, min=-reach, max=reach).astype(dtype)


def setup_inputs(seed: int = 0, part: int = 0) -> dict:
    streams_of = jax.random.split(jax.random.key(seed), 7)
    part_keys = jax.random.split(jax.random.fold_in(streams_of[6], part), 7)
    return {
        "activations": draw_activations(jax.random.fold_in(jax.random.fold_in(streams_of[6], part), 71), part),
        "cotangent": normal_values(part_keys[1], (WINDOWS, WINDOW_BINS, CHANNELS), 1.0, 6.0, ((0, 2), (1, 8))),
        "conv_one": normal_values(streams_of[2], (CHANNELS, 3, MIDDLE), (3 * CHANNELS) ** -0.5, 0.109375, ((0, 16),)),
        "mix_one": normal_values(streams_of[3], (MIDDLE, CHANNELS), MIDDLE ** -0.5, 0.25, ((0, 16),)),
        "conv_two": normal_values(streams_of[4], (CHANNELS, 3, MIDDLE), (3 * CHANNELS) ** -0.5, 0.109375, ((0, 16),)),
        "mix_two": normal_values(streams_of[5], (MIDDLE, CHANNELS), MIDDLE ** -0.5, 0.25, ((0, 16),)),
    }


def prenorm(values):
    scale = lax.rsqrt(lax.optimization_barrier(jnp.mean(values * values, axis=-1, keepdims=True)) + 1e-06)
    return jax.nn.gelu(values * scale)

def shifted(field, dilate):
    length = field.shape[1]
    padded = jnp.pad(field, ((0, 0), (dilate, dilate), (0, 0)))
    return [padded[:, tap * dilate:tap * dilate + length] for tap in range(3)]

def forward(inputs, conv_w, mix_w, dilate):
    width = inputs.shape[-1]
    normed = prenorm(inputs.astype(jnp.float32)).astype(jnp.bfloat16)
    views = shifted(normed, dilate)
    preact = jnp.dot(views[0].reshape(-1, width), conv_w[:, 0, :], preferred_element_type=jnp.float32)
    for tap in range(1, 3):
        preact = preact + jnp.dot(views[tap].reshape(-1, width), conv_w[:, tap, :], preferred_element_type=jnp.float32)
    hidden = jax.nn.gelu(preact).astype(jnp.bfloat16)
    mixed = inputs.reshape(-1, width).astype(jnp.float32) + jnp.dot(hidden, mix_w, preferred_element_type=jnp.float32)
    return (mixed.astype(jnp.bfloat16).reshape(inputs.shape), normed, preact, hidden)

def backward(inputs, normed, preact, hidden, upstream, conv_w, mix_w, dilate):
    width = inputs.shape[-1]
    middle = mix_w.shape[0]
    flat_up = upstream.reshape(-1, width)
    grad_mix = jnp.dot(hidden.T, flat_up, preferred_element_type=jnp.float32)
    dhidden = jnp.dot(flat_up, mix_w.T, preferred_element_type=jnp.float32)
    unused, pull = jax.vjp(jax.nn.gelu, preact)
    dpre = pull(dhidden)[0].astype(jnp.bfloat16)
    views = shifted(normed, dilate)
    grad_conv = jnp.stack([jnp.dot(views[tap].reshape(-1, width).T, dpre, preferred_element_type=jnp.float32) for tap in range(3)], axis=1)
    back_views = shifted(dpre.reshape(inputs.shape[0], inputs.shape[1], middle), dilate)
    dnormed = jnp.dot(back_views[2].reshape(-1, middle), conv_w[:, 0, :].T, preferred_element_type=jnp.float32)
    for tap in range(1, 3):
        dnormed = dnormed + jnp.dot(back_views[2 - tap].reshape(-1, middle), conv_w[:, tap, :].T, preferred_element_type=jnp.float32)
    unused_two, pull_norm = jax.vjp(prenorm, inputs.astype(jnp.float32))
    dinput = pull_norm(dnormed.reshape(inputs.shape))[0]
    result = (upstream.astype(jnp.float32) + dinput).astype(jnp.bfloat16)
    return (result, grad_conv, grad_mix)

def reference(activations, cotangent, conv_one, mix_one, conv_two, mix_two):
    second_in, normed_one, preact_one, hidden_one = forward(activations, conv_one, mix_one, DILATE_ONE)
    unused, normed_two, preact_two, hidden_two = forward(second_in, conv_two, mix_two, DILATE_TWO)
    upstream, grad_conv_two, grad_mix_two = backward(second_in, normed_two, preact_two, hidden_two, cotangent, conv_two, mix_two, DILATE_TWO)
    input_grad, grad_conv_one, grad_mix_one = backward(activations, normed_one, preact_one, hidden_one, upstream, conv_one, mix_one, DILATE_ONE)
    return (input_grad, grad_conv_one, grad_mix_one, grad_conv_two, grad_mix_two)
```

```python
import functools
import math

import jax
import jax.numpy as jnp
from jax import lax
from jax.experimental import pallas as pl
from jax.experimental.pallas import tpu as pltpu
from jax.sharding import PartitionSpec as P

DILATE_ONE = 64
DILATE_TWO = 128
BF = jnp.bfloat16
F32 = jnp.float32
ROOT = math.sqrt(2.0 / math.pi)
CUBE = 0.044715
VMEM = pl.BlockSpec(memory_space=pltpu.VMEM)
ANY = pl.BlockSpec(memory_space=pl.ANY)
NT = (((1,), (1,)), ((), ()))
TN = (((0,), (0,)), ((), ()))


def gelu(v):
    return v * (0.5 * (1.0 + jnp.tanh(ROOT * (v + CUBE * (v * v * v)))))


def gelu_slope(v):
    t = jnp.tanh(ROOT * (v + CUBE * (v * v * v)))
    return 0.5 * (1.0 + t) + (0.5 * v) * (1.0 - t * t) * (ROOT * (1.0 + 3.0 * CUBE * (v * v)))


def norm_scale(v):
    return lax.rsqrt(jnp.mean(v * v, axis=-1, keepdims=True) + 1e-06)


def dot(a, b, dims=(((1,), (0,)), ((), ()))):
    return lax.dot_general(a, b, dims, preferred_element_type=F32)


def params():
    return pltpu.CompilerParams(vmem_limit_bytes=40 << 20)


def swap(value, axis, bit):
    count = lax.axis_size(axis)
    return lax.ppermute(value, axis, [(i, i ^ bit) for i in range(count)])


def step_orders(count):
    bits = [1 << i for i in reversed(range(count.bit_length() - 1))]
    assert math.prod([2] * len(bits)) == count
    return bits, bits[-1:] + bits[:-1]


def offset_of(index, steps):
    return sum(step for j, step in enumerate(steps) if (index >> j) & 1)


def place_of(offset, steps):
    place = 0
    for j, step in enumerate(steps):
        shift = step.bit_length() - 1
        place = place + (((offset >> shift) & 1) << j)
    return place


def gather_pair(first, second, orders):
    one, two = first[None], second[None]
    for left, right in zip(*orders):
        got_one = swap(one, "seq", left)
        got_two = swap(two, "seq", right)
        one = jnp.concatenate([one, got_one], axis=0)
        two = jnp.concatenate([two, got_two], axis=0)
    return one, swap(one, "dp", 1), two, swap(two, "dp", 1)


def scatter_sum(keep, send, steps):
    total = keep + swap(send, "dp", 1).astype(F32)
    for step in reversed(steps):
        half = total.shape[0] // 2
        got = swap(total[half:].astype(BF), "seq", step)
        total = total[:half] + got.astype(F32)
    return total[0]


def halo(first, last):
    count = lax.axis_size("seq")
    low = lax.ppermute(last, "seq", [(i, i + 1) for i in range(count - 1)])
    high = lax.ppermute(first, "seq", [(i + 1, i) for i in range(count - 1)])
    return low, high


def fetch_weights(orders, pieces, taps, rest, sem):
    here, core = lax.axis_index("seq"), lax.axis_index("dp")
    copies = []
    for which, (target, steps) in enumerate(((taps, orders[0]), (rest, orders[1]))):
        own, other = pieces[2 * which], pieces[2 * which + 1]
        for index in range(own.shape[0]):
            where = here ^ offset_of(index, steps)
            for piece, lane in ((own, core), (other, 1 - core)):
                copy = pltpu.make_async_copy(
                    piece.at[index], target.at[where, lane], sem.at[len(copies)]
                )
                copy.start()
                copies.append(copy)
    return copies


def weight_scratch(count, rows, width):
    return [
        pltpu.VMEM((count, 2, rows, width), BF),
        pltpu.VMEM((count, 2, rows, width), BF),
        pltpu.SemaphoreType.DMA((4 * count,)),
    ]


def conv_weights(taps, rest, middle):
    rows = taps.shape[0] * taps.shape[1] * taps.shape[2]
    return [
        taps[:, :, :, :middle].reshape(rows, middle),
        taps[:, :, :, middle:].reshape(rows, middle),
        rest[:, :, :, :middle].reshape(rows, middle),
    ]


def mix_halves(rest, middle):
    half = rest.shape[2] // 2
    return [
        rest[:, :, :half, middle:].reshape(middle, middle),
        rest[:, :, half:, middle:].reshape(middle, middle),
    ]


def norm_kernel(x_ref, low_ref, high_ref, ext_ref):
    dilate = low_ref.shape[1]
    length = x_ref.shape[1]
    for w in range(x_ref.shape[0]):
        for source, start, size in (
            (low_ref, 0, dilate),
            (x_ref, dilate, length),
            (high_ref, dilate + length, dilate),
        ):

            @pl.loop(0, size // 32)
            def _(i):
                rows = pl.multiple_of(i * 32, 32)
                v = source[w, pl.ds(rows, 32), :].astype(F32)
                ext_ref[w, pl.ds(start + rows, 32), :] = gelu(v * norm_scale(v)).astype(BF)


def norm_ext(x, low, high):
    windows, length, width = x.shape
    return pl.pallas_call(
        norm_kernel,
        out_shape=jax.ShapeDtypeStruct((windows, length + 2 * low.shape[1], width), BF),
        in_specs=[VMEM] * 3,
        out_specs=VMEM,
        compiler_params=params(),
        name="norm_ext",
    )(x, low, high)


def forward_kernel(
    orders, dilate, edge, ext, x_ref, a0, a1, b0, b1,
    pre_ref, hid_ref, x2_ref, first_ref, last_ref, taps, rest, sem,
):
    copies = fetch_weights(orders, (a0, a1, b0, b1), taps, rest, sem)
    for copy in copies:
        copy.wait()
    windows, length, width = x_ref.shape
    middle = hid_ref.shape[1]
    conv = conv_weights(taps, rest, middle)
    mix = mix_halves(rest, middle)
    for w in range(windows):
        pre = sum(dot(ext[w, k * dilate : k * dilate + length, :], conv[k]) for k in range(3))
        pre_ref[w * length : (w + 1) * length, :] = pre
        hid_ref[w * length : (w + 1) * length, :] = gelu(pre).astype(BF)
        hid = hid_ref[w * length : (w + 1) * length, :]
        for h in range(2):
            cols = slice(h * middle, (h + 1) * middle)
            x2_ref[w, :, cols] = (x_ref[w, :, cols].astype(F32) + dot(hid, mix[h])).astype(BF)
        for target, start in ((first_ref, 0), (last_ref, length - edge)):

            @pl.loop(0, edge // 32)
            def _(i):
                rows = pl.multiple_of(i * 32, 32)
                v = x2_ref[w, pl.ds(start + rows, 32), :].astype(F32)
                target[w, pl.ds(rows, 32), :] = gelu(v * norm_scale(v)).astype(BF)


def forward_block(ext, x, pieces, orders, dilate, edge):
    windows, length, width = x.shape
    count, rows, packed = pieces[0].shape
    middle = packed // 2
    flat = windows * length
    return pl.pallas_call(
        functools.partial(forward_kernel, orders, dilate, edge),
        out_shape=(
            jax.ShapeDtypeStruct((flat, middle), F32),
            jax.ShapeDtypeStruct((flat, middle), BF),
            jax.ShapeDtypeStruct(x.shape, BF),
            jax.ShapeDtypeStruct((windows, edge, width), BF),
            jax.ShapeDtypeStruct((windows, edge, width), BF),
        ),
        in_specs=[VMEM, VMEM] + [ANY] * 4,
        out_specs=(VMEM,) * 5,
        scratch_shapes=weight_scratch(count, rows, packed),
        compiler_params=params(),
        cost_estimate=pl.CostEstimate(
            flops=8 * flat * width * middle, bytes_accessed=16 << 20, transcendentals=0
        ),
        name="forward_block",
    )(ext, x, *pieces)


def turn_kernel(
    orders, dilate, first, last, low, high, e_ref, a0, a1, b0, b1,
    ext, hid_ref, dpre_ref, dfirst, dlast, taps, rest, sem,
):
    copies = fetch_weights(orders, (a0, a1, b0, b1), taps, rest, sem)
    windows, length, width = e_ref.shape
    edge = first.shape[1]
    middle = hid_ref.shape[1]
    for w in range(windows):
        for source, start in (
            (low, 0), (first, dilate), (last, dilate + length - edge), (high, dilate + length),
        ):
            ext[w, start : start + edge, :] = source[w]
    for copy in copies:
        copy.wait()
    conv = conv_weights(taps, rest, middle)
    mix = mix_halves(rest, middle)
    for w in range(windows):
        pre = sum(dot(ext[w, k * dilate : k * dilate + length, :], conv[k]) for k in range(3))
        dhid = dot(e_ref[w, :, :middle], mix[0], NT) + dot(e_ref[w, :, middle:], mix[1], NT)
        rows = slice(w * length, (w + 1) * length)
        hid_ref[rows, :] = gelu(pre).astype(BF)
        dpre_ref[rows, :] = (gelu_slope(pre) * dhid).astype(BF)
        dfirst[w] = dpre_ref[w * length : w * length + dilate, :]
        dlast[w] = dpre_ref[(w + 1) * length - dilate : (w + 1) * length, :]


def turn_block(first, last, low, high, e, pieces, orders, dilate):
    windows, length, width = e.shape
    count, rows, packed = pieces[0].shape
    middle = packed // 2
    flat = windows * length
    return pl.pallas_call(
        functools.partial(turn_kernel, orders, dilate),
        out_shape=(
            jax.ShapeDtypeStruct((windows, length + 2 * dilate, width), BF),
            jax.ShapeDtypeStruct((flat, middle), BF),
            jax.ShapeDtypeStruct((flat, middle), BF),
            jax.ShapeDtypeStruct((windows, dilate, middle), BF),
            jax.ShapeDtypeStruct((windows, dilate, middle), BF),
        ),
        in_specs=[VMEM] * 5 + [ANY] * 4,
        out_specs=(VMEM,) * 5,
        scratch_shapes=weight_scratch(count, rows, packed),
        compiler_params=params(),
        cost_estimate=pl.CostEstimate(
            flops=8 * flat * width * middle, bytes_accessed=16 << 20, transcendentals=0
        ),
        name="turn_block",
    )(first, last, low, high, e, *pieces)


def grads_kernel(orders, dilate, ext, hid, e_ref, dpre, keep_a, send_a, keep_b, send_b, full):
    here, core = lax.axis_index("seq"), lax.axis_index("dp")
    windows, length, width = e_ref.shape
    middle = hid.shape[1]
    count, rows, packed = keep_a.shape
    half = rows // 2
    for k in (2, 0, 1, 3):
        if k == 3:
            for h in range(2):
                e = jnp.concatenate(
                    [e_ref[w, :, h * middle : (h + 1) * middle] for w in range(windows)], axis=0
                )
                full[h * middle : (h + 1) * middle, :] = dot(hid[...], e, TN)
        else:
            view = jnp.concatenate(
                [ext[w, k * dilate : k * dilate + length, :] for w in range(windows)], axis=0
            )
            full[...] = dot(view, dpre[...], TN)
        keep, send, steps = (
            (keep_a, send_a, orders[0]) if k < 2 else (keep_b, send_b, orders[1])
        )
        cols = slice((k % 2) * middle, (k % 2 + 1) * middle)
        for chip in range(count):
            place = place_of(here ^ chip, steps)
            if k == 3:
                for h in range(2):
                    base = h * middle + chip * rows
                    out = slice(h * half, (h + 1) * half)
                    mine = full[pl.ds(pl.multiple_of(base + core * half, half), half), :]
                    theirs = full[pl.ds(pl.multiple_of(base + (1 - core) * half, half), half), :]
                    keep[place, out, cols] = mine
                    send[place, out, cols] = theirs.astype(BF)
            else:
                base = 2 * chip * rows
                mine = full[pl.ds(pl.multiple_of(base + core * rows, rows), rows), :]
                theirs = full[pl.ds(pl.multiple_of(base + (1 - core) * rows, rows), rows), :]
                keep[place, :, cols] = mine
                send[place, :, cols] = theirs.astype(BF)


def grads_block(ext, hid, e, dpre, orders, dilate, count):
    windows, length, width = e.shape
    flat, middle = hid.shape
    rows = width // (2 * count)
    shape = (count, rows, 2 * middle)
    return pl.pallas_call(
        functools.partial(grads_kernel, orders, dilate),
        out_shape=(
            jax.ShapeDtypeStruct(shape, F32),
            jax.ShapeDtypeStruct(shape, BF),
            jax.ShapeDtypeStruct(shape, F32),
            jax.ShapeDtypeStruct(shape, BF),
        ),
        in_specs=[VMEM] * 4,
        out_specs=(VMEM,) * 4,
        scratch_shapes=[pltpu.VMEM((width, middle), F32)],
        compiler_params=params(),
        cost_estimate=pl.CostEstimate(
            flops=8 * flat * width * middle, bytes_accessed=16 << 20, transcendentals=0
        ),
        name="grads_block",
    )(ext, hid, e, dpre)


def back_kernel(orders, dilate, chained, *refs):
    dpre, low, high, x_ref, e_ref, a0, a1, b0, b1 = refs[:9]
    if chained:
        (m0, m1, pre_ref, out_ref, dprev, dfirst, dlast) = refs[9:16]
        ext, dn, taps, rest, sem, taps_m, rest_m, sem_m = refs[16:]
    else:
        out_ref = refs[9]
        ext, dn, taps, rest, sem = refs[10:]
    copies = fetch_weights(orders, (a0, a1, b0, b1), taps, rest, sem)
    windows, length, width = x_ref.shape
    middle = dpre.shape[1]
    if chained:
        here, core = lax.axis_index("seq"), lax.axis_index("dp")
        for index in range(m0.shape[0]):
            where = here ^ offset_of(index, orders[1])
            for j, (piece, lane) in enumerate(((m0, core), (m1, 1 - core))):
                copy = pltpu.make_async_copy(
                    piece.at[index], rest_m.at[where, lane], sem_m.at[2 * index + j]
                )
                copy.start()
                copies.append(copy)
    for w in range(windows):
        ext[w, :dilate, :] = low[w]
        ext[w, dilate : dilate + length, :] = dpre[w * length : (w + 1) * length, :]
        ext[w, dilate + length :, :] = high[w]
    for copy in copies:
        copy.wait()
    conv = conv_weights(taps, rest, middle)
    for w in range(windows):
        dn[...] = sum(
            dot(ext[w, (2 - k) * dilate : (2 - k) * dilate + length, :], conv[k], NT)
            for k in range(3)
        )

        @pl.loop(0, length // 32)
        def _(i):
            rows = pl.ds(pl.multiple_of(i * 32, 32), 32)
            v = x_ref[w, rows, :].astype(F32)
            scale = norm_scale(v)
            u = v * scale
            g = dn[rows, :] * gelu_slope(u)
            dv = scale * (g - u * jnp.mean(g * u, axis=-1, keepdims=True))
            out_ref[w, rows, :] = (e_ref[w, rows, :].astype(F32) + dv).astype(BF)

        if chained:
            mix = mix_halves(rest_m, middle)
            edge = dfirst.shape[1]
            dhid = dot(out_ref[w, :, :middle], mix[0], NT) + dot(out_ref[w, :, middle:], mix[1], NT)
            rows = slice(w * length, (w + 1) * length)
            dprev[rows, :] = (gelu_slope(pre_ref[rows, :]) * dhid).astype(BF)
            dfirst[w] = dprev[w * length : w * length + edge, :]
            dlast[w] = dprev[(w + 1) * length - edge : (w + 1) * length, :]


def back_block(dpre, low, high, x, e, pieces, orders, dilate, previous=None):
    windows, length, width = x.shape
    count, rows, packed = pieces[0].shape
    flat, middle = dpre.shape
    chained = previous is not None
    operands = [dpre, low, high, x, e, *pieces]
    in_specs = [VMEM] * 5 + [ANY] * 4
    shapes = [jax.ShapeDtypeStruct(x.shape, BF)]
    scratch = [
        pltpu.VMEM((windows, length + 2 * dilate, middle), BF),
        pltpu.VMEM((length, width), F32),
    ] + weight_scratch(count, rows, packed)
    if chained:
        others, pre, edge = previous
        operands += [others[2], others[3], pre]
        in_specs += [ANY, ANY, VMEM]
        shapes += [
            jax.ShapeDtypeStruct((flat, middle), BF),
            jax.ShapeDtypeStruct((windows, edge, middle), BF),
            jax.ShapeDtypeStruct((windows, edge, middle), BF),
        ]
        scratch += [pltpu.VMEM((8, 128), BF)] + weight_scratch(count, rows, packed)[1:]
    return pl.pallas_call(
        functools.partial(back_kernel, orders, dilate, chained),
        out_shape=tuple(shapes),
        in_specs=in_specs,
        out_specs=(VMEM,) * len(shapes),
        scratch_shapes=scratch,
        compiler_params=params(),
        cost_estimate=pl.CostEstimate(
            flops=8 * flat * width * middle, bytes_accessed=16 << 20, transcendentals=0
        ),
        name="back_block",
    )(*operands)


def pack(conv, mix):
    middle = conv.shape[2]
    first = conv[:, :2].reshape(conv.shape[0], 2 * middle)
    tall = jnp.concatenate([mix[:, :middle], mix[:, middle:]], axis=0)
    second = jnp.concatenate([conv[:, 2], tall], axis=1)
    return first, second


def unpack(first, second, middle):
    rows = first.shape[0]
    conv = jnp.concatenate(
        [first.reshape(rows, 2, middle), second[:, None, :middle]], axis=1
    )
    half = rows // 2
    mix = jnp.concatenate([second[:half, middle:], second[half:, middle:]], axis=1)
    return conv, mix


def body(activations, cotangent, conv_one, mix_one, conv_two, mix_two):
    count = lax.axis_size("seq")
    orders = step_orders(count)
    middle = conv_one.shape[2]
    length = activations.shape[1]
    low, high = halo(
        activations[:, :DILATE_ONE], activations[:, length - DILATE_ONE :]
    )
    pieces_one = gather_pair(*pack(conv_one, mix_one), orders)
    pieces_two = gather_pair(*pack(conv_two, mix_two), orders)
    ext_one = norm_ext(activations, low, high)
    pre_one, hid_one, second_in, first, last = forward_block(
        ext_one, activations, pieces_one, orders, DILATE_ONE, DILATE_TWO
    )
    low, high = halo(first, last)
    ext_two, hid_two, dpre_two, dfirst, dlast = turn_block(
        first, last, low, high, cotangent, pieces_two, orders, DILATE_TWO
    )
    dlow, dhigh = halo(dfirst, dlast)
    ka, sa, kb, sb = grads_block(ext_two, hid_two, cotangent, dpre_two, orders, DILATE_TWO, count)
    grads_two = unpack(scatter_sum(ka, sa, orders[0]), scatter_sum(kb, sb, orders[1]), middle)
    upstream, dpre_one, dfirst, dlast = back_block(
        dpre_two, dlow, dhigh, second_in, cotangent, pieces_two, orders, DILATE_TWO,
        (pieces_one, pre_one, DILATE_ONE),
    )
    dlow, dhigh = halo(dfirst, dlast)
    ka, sa, kb, sb = grads_block(ext_one, hid_one, upstream, dpre_one, orders, DILATE_ONE, count)
    grads_one = unpack(scatter_sum(ka, sa, orders[0]), scatter_sum(kb, sb, orders[1]), middle)
    (input_grad,) = back_block(
        dpre_one, dlow, dhigh, activations, upstream, pieces_one, orders, DILATE_ONE
    )
    return (input_grad, *grads_one, *grads_two)


def solution(mesh):
    in_specs = (
        P(("parts", "dp"), "seq", None),
        P(("parts", "dp"), "seq", None),
        P(("seq", "dp"), None, None),
        P(("seq", "dp"), None),
        P(("seq", "dp"), None, None),
        P(("seq", "dp"), None),
    )
    out_specs = (
        P(("parts", "dp"), "seq", None),
        P(("parts", "seq", "dp"), None, None),
        P(("parts", "seq", "dp"), None),
        P(("parts", "seq", "dp"), None, None),
        P(("parts", "seq", "dp"), None),
    )
    return jax.shard_map(body, mesh=mesh, in_specs=in_specs, out_specs=out_specs, check_vma=False)
```

```python
import functools
import math

import jax
import jax.numpy as jnp
from jax import lax
from jax.experimental import pallas as pl
from jax.experimental.pallas import tpu as pltpu
from jax.sharding import PartitionSpec as P

DILATE_ONE = 64
DILATE_TWO = 128
BF = jnp.bfloat16
F32 = jnp.float32
ROOT = math.sqrt(2.0 / math.pi)
CUBE = 0.044715
VMEM = pl.BlockSpec(memory_space=pltpu.VMEM)
NT = (((1,), (1,)), ((), ()))
TN = (((0,), (0,)), ((), ()))


def gelu(v):
    return v * (0.5 * (1.0 + jnp.tanh(ROOT * (v + CUBE * (v * v * v)))))


def gelu_slope(v):
    t = jnp.tanh(ROOT * (v + CUBE * (v * v * v)))
    return 0.5 * (1.0 + t) + (0.5 * v) * (1.0 - t * t) * (ROOT * (1.0 + 3.0 * CUBE * (v * v)))


def norm_scale(v):
    return lax.rsqrt(jnp.mean(v * v, axis=-1, keepdims=True) + 1e-06)


def dot(a, b, dims=(((1,), (0,)), ((), ()))):
    return lax.dot_general(a, b, dims, preferred_element_type=F32)


def cost(flat, width, middle):
    return pl.CostEstimate(
        flops=8 * flat * width * middle, bytes_accessed=8 << 20, transcendentals=0
    )


def params():
    return pltpu.CompilerParams(vmem_limit_bytes=40 << 20)


def tie(*values):
    return lax.optimization_barrier(values)


def step_orders(count):
    bits = [1 << i for i in reversed(range(count.bit_length() - 1))]
    assert math.prod([2] * len(bits)) == count
    return bits, bits[-1:] + bits[:-1]


def place_of(offset, steps):
    place = 0
    for j, step in enumerate(steps):
        shift = step.bit_length() - 1
        place = place + (((offset >> shift) & 1) << j)
    return place


def cross(value):
    return lax.ppermute(value, "dp", [(0, 1), (1, 0)])


def hop(value, orders, j):
    count = lax.axis_size("seq")
    pairs = [
        (2 * i + core, 2 * (i ^ orders[core][j]) + core)
        for i in range(count)
        for core in range(2)
    ]
    return lax.ppermute(value, ("seq", "dp"), pairs)


def widen(value, orders, j):
    return jnp.concatenate([value, hop(value, orders, j)], axis=0)


def fold(total, orders, j):
    half = total.shape[0] // 2
    return total[:half] + hop(total[half:].astype(BF), orders, j).astype(F32)


def halo(first, last):
    count = lax.axis_size("seq")
    low = lax.ppermute(last, "seq", [(i, i + 1) for i in range(count - 1)])
    high = lax.ppermute(first, "seq", [(i + 1, i) for i in range(count - 1)])
    return low, high


def by_core(own, other, run):
    core = lax.axis_index("dp")

    @pl.when(core == 0)
    def _():
        run(own, other)

    @pl.when(core == 1)
    def _():
        run(other, own)


def conv_weights(orders, taps, rest, middle):
    here = lax.axis_index("seq")
    count = taps.shape[0]

    def whole(ref, steps, half):
        cols = slice(half * middle, (half + 1) * middle)
        return jnp.concatenate(
            [ref[place_of(here ^ chip, steps), :, cols] for chip in range(count)], axis=0
        )

    return [
        lambda: whole(taps, orders[0], 0),
        lambda: whole(taps, orders[0], 1),
        lambda: whole(rest, orders[1], 0),
    ]


def mix_halves(orders, rest, middle):
    here = lax.axis_index("seq")
    count, rows = rest.shape[:2]
    part = rows // 4

    def half(h):
        pieces = []
        for chip in range(count):
            place = place_of(here ^ chip, orders[1])
            for lane in range(2):
                start = (2 * lane + h) * part
                pieces.append(rest[place, start : start + part, middle:])
        return jnp.concatenate(pieces, axis=0)

    return [lambda: half(0), lambda: half(1)]


def norm_kernel(x_ref, low_ref, high_ref, ext_ref):
    dilate = low_ref.shape[1]
    length = x_ref.shape[1]
    for w in range(x_ref.shape[0]):
        for source, start, size in (
            (low_ref, 0, dilate),
            (x_ref, dilate, length),
            (high_ref, dilate + length, dilate),
        ):

            @pl.loop(0, size // 32)
            def _(i):
                rows = pl.multiple_of(i * 32, 32)
                v = source[w, pl.ds(rows, 32), :].astype(F32)
                ext_ref[w, pl.ds(start + rows, 32), :] = gelu(v * norm_scale(v)).astype(BF)


def norm_ext(x, low, high):
    windows, length, width = x.shape
    return pl.pallas_call(
        norm_kernel,
        out_shape=jax.ShapeDtypeStruct((windows, length + 2 * low.shape[1], width), BF),
        in_specs=[VMEM] * 3,
        out_specs=VMEM,
        compiler_params=params(),
        name="norm_ext",
    )(x, low, high)


def forward_kernel(
    orders, dilate, edge, ext, x_ref, own, other, pre_ref, hid_ref, x2_ref, first_ref, last_ref
):
    windows, length, width = x_ref.shape
    middle = hid_ref.shape[1]

    def run(taps, rest):
        conv = conv_weights(orders, taps, rest, middle)
        mix = mix_halves(orders, rest, middle)
        for w in range(windows):
            rows = slice(w * length, (w + 1) * length)
            pre = sum(dot(ext[w, k * dilate : k * dilate + length, :], conv[k]()) for k in range(3))
            pre_ref[rows, :] = pre
            hid = gelu(pre).astype(BF)
            hid_ref[rows, :] = hid
            for h in range(2):
                cols = slice(h * middle, (h + 1) * middle)
                x2_ref[w, :, cols] = (x_ref[w, :, cols].astype(F32) + dot(hid, mix[h]())).astype(BF)

    by_core(own, other, run)
    for w in range(windows):
        for target, start in ((first_ref, 0), (last_ref, length - edge)):

            @pl.loop(0, edge // 32)
            def _(i):
                rows = pl.multiple_of(i * 32, 32)
                v = x2_ref[w, pl.ds(start + rows, 32), :].astype(F32)
                target[w, pl.ds(rows, 32), :] = gelu(v * norm_scale(v)).astype(BF)


def forward_block(ext, x, pieces, orders, dilate, edge):
    windows, length, width = x.shape
    middle = pieces[0].shape[2] // 2
    flat = windows * length
    return pl.pallas_call(
        functools.partial(forward_kernel, orders, dilate, edge),
        out_shape=(
            jax.ShapeDtypeStruct((flat, middle), F32),
            jax.ShapeDtypeStruct((flat, middle), BF),
            jax.ShapeDtypeStruct(x.shape, BF),
            jax.ShapeDtypeStruct((windows, edge, width), BF),
            jax.ShapeDtypeStruct((windows, edge, width), BF),
        ),
        in_specs=[VMEM] * 4,
        out_specs=(VMEM,) * 5,
        compiler_params=params(),
        cost_estimate=cost(flat, width, middle),
        name="forward_block",
    )(ext, x, *pieces)


def turn_kernel(
    orders, dilate, first, last, low, high, e_ref, own, other,
    ext, hid_ref, dpre_ref, dfirst, dlast,
):
    windows, length, width = e_ref.shape
    edge = first.shape[1]
    middle = hid_ref.shape[1]
    for w in range(windows):
        for source, start in (
            (low, 0), (first, dilate), (last, dilate + length - edge), (high, dilate + length),
        ):
            ext[w, start : start + edge, :] = source[w]

    def run(taps, rest):
        conv = conv_weights(orders, taps, rest, middle)
        mix = mix_halves(orders, rest, middle)
        for w in range(windows):
            rows = slice(w * length, (w + 1) * length)
            pre = sum(dot(ext[w, k * dilate : k * dilate + length, :], conv[k]()) for k in range(3))
            dhid = dot(e_ref[w, :, :middle], mix[0](), NT) + dot(e_ref[w, :, middle:], mix[1](), NT)
            hid_ref[rows, :] = gelu(pre).astype(BF)
            dpre_ref[rows, :] = (gelu_slope(pre) * dhid).astype(BF)

    by_core(own, other, run)
    for w in range(windows):
        dfirst[w] = dpre_ref[w * length : w * length + dilate, :]
        dlast[w] = dpre_ref[(w + 1) * length - dilate : (w + 1) * length, :]


def turn_block(first, last, low, high, e, pieces, orders, dilate):
    windows, length, width = e.shape
    middle = pieces[0].shape[2] // 2
    flat = windows * length
    return pl.pallas_call(
        functools.partial(turn_kernel, orders, dilate),
        out_shape=(
            jax.ShapeDtypeStruct((windows, length + 2 * dilate, width), BF),
            jax.ShapeDtypeStruct((flat, middle), BF),
            jax.ShapeDtypeStruct((flat, middle), BF),
            jax.ShapeDtypeStruct((windows, dilate, middle), BF),
            jax.ShapeDtypeStruct((windows, dilate, middle), BF),
        ),
        in_specs=[VMEM] * 7,
        out_specs=(VMEM,) * 5,
        compiler_params=params(),
        cost_estimate=cost(flat, width, middle),
        name="turn_block",
    )(first, last, low, high, e, *pieces)


def grads_kernel(orders, dilate, ext, hid, e_ref, dpre, keep, send, full):
    here, core = lax.axis_index("seq"), lax.axis_index("dp")
    windows, length, width = e_ref.shape
    middle = hid.shape[1]
    count, rows = keep.shape[:2]
    part = rows // 4

    def put(target, k):
        steps = orders[k // 2]
        cols = slice((k % 2) * middle, (k % 2 + 1) * middle)
        for chip in range(count):
            place = place_of(here ^ chip, steps)
            if k < 3:
                value = full[chip * rows : (chip + 1) * rows, :]
                target[place, :, cols] = value.astype(target.dtype)
                continue
            for lane in range(2):
                for h in range(2):
                    base = h * middle + (2 * chip + lane) * part
                    start = (2 * lane + h) * part
                    value = full[base : base + part, :]
                    target[place, start : start + part, cols] = value.astype(target.dtype)

    for k in range(4):
        if k == 3:
            for h in range(2):
                e = jnp.concatenate(
                    [e_ref[w, :, h * middle : (h + 1) * middle] for w in range(windows)], axis=0
                )
                full[h * middle : (h + 1) * middle, :] = dot(hid[...], e, TN)
        else:
            view = jnp.concatenate(
                [ext[w, k * dilate : k * dilate + length, :] for w in range(windows)], axis=0
            )
            full[...] = dot(view, dpre[...], TN)

        @pl.when(core == k // 2)
        def _():
            put(keep, k)

        @pl.when(core != k // 2)
        def _():
            put(send, k)


def grads_block(ext, hid, e, dpre, orders, dilate, count):
    windows, length, width = e.shape
    flat, middle = hid.shape
    shape = (count, width // count, 2 * middle)
    return pl.pallas_call(
        functools.partial(grads_kernel, orders, dilate),
        out_shape=(jax.ShapeDtypeStruct(shape, F32), jax.ShapeDtypeStruct(shape, BF)),
        in_specs=[VMEM] * 4,
        out_specs=(VMEM,) * 2,
        scratch_shapes=[pltpu.VMEM((width, middle), F32)],
        compiler_params=params(),
        cost_estimate=cost(flat, width, middle),
        name="grads_block",
    )(ext, hid, e, dpre)


def back_kernel(orders, dilate, chained, *refs):
    dpre, low, high, x_ref, e_ref, own, other = refs[:7]
    if chained:
        own_m, other_m, pre_ref, out_ref, dprev, dfirst, dlast, ext, dn = refs[7:]
    else:
        out_ref, ext, dn = refs[7:]
    windows, length, width = x_ref.shape
    middle = dpre.shape[1]
    for w in range(windows):
        ext[w, :dilate, :] = low[w]
        ext[w, dilate : dilate + length, :] = dpre[w * length : (w + 1) * length, :]
        ext[w, dilate + length :, :] = high[w]

    def run(taps, rest):
        conv = conv_weights(orders, taps, rest, middle)
        for w in range(windows):
            dn[w] = sum(
                dot(ext[w, (2 - k) * dilate : (2 - k) * dilate + length, :], conv[k](), NT)
                for k in range(3)
            )

    by_core(own, other, run)
    for w in range(windows):

        @pl.loop(0, length // 32)
        def _(i):
            rows = pl.ds(pl.multiple_of(i * 32, 32), 32)
            v = x_ref[w, rows, :].astype(F32)
            scale = norm_scale(v)
            u = v * scale
            g = dn[w, rows, :] * gelu_slope(u)
            dv = scale * (g - u * jnp.mean(g * u, axis=-1, keepdims=True))
            out_ref[w, rows, :] = (e_ref[w, rows, :].astype(F32) + dv).astype(BF)

    if chained:

        def turn(taps, rest):
            mix = mix_halves(orders, rest, middle)
            for w in range(windows):
                dhid = dot(out_ref[w, :, :middle], mix[0](), NT) + dot(
                    out_ref[w, :, middle:], mix[1](), NT
                )
                rows = slice(w * length, (w + 1) * length)
                dprev[rows, :] = (gelu_slope(pre_ref[rows, :]) * dhid).astype(BF)

        by_core(own_m, other_m, turn)
        edge = dfirst.shape[1]
        for w in range(windows):
            dfirst[w] = dprev[w * length : w * length + edge, :]
            dlast[w] = dprev[(w + 1) * length - edge : (w + 1) * length, :]


def back_block(dpre, low, high, x, e, pieces, orders, dilate, previous=None):
    windows, length, width = x.shape
    flat, middle = dpre.shape
    chained = previous is not None
    operands = [dpre, low, high, x, e, *pieces]
    shapes = [jax.ShapeDtypeStruct(x.shape, BF)]
    if chained:
        others, pre, edge = previous
        operands += [*others, pre]
        shapes += [
            jax.ShapeDtypeStruct((flat, middle), BF),
            jax.ShapeDtypeStruct((windows, edge, middle), BF),
            jax.ShapeDtypeStruct((windows, edge, middle), BF),
        ]
    return pl.pallas_call(
        functools.partial(back_kernel, orders, dilate, chained),
        out_shape=tuple(shapes),
        in_specs=[VMEM] * len(operands),
        out_specs=(VMEM,) * len(shapes),
        scratch_shapes=[
            pltpu.VMEM((windows, length + 2 * dilate, middle), BF),
            pltpu.VMEM((windows, length, width), F32),
        ],
        compiler_params=params(),
        cost_estimate=cost(flat, width, middle),
        name="back_block",
    )(*operands)


def pack(conv, mix):
    middle = conv.shape[2]
    first = conv[:, :2].reshape(conv.shape[0], 2 * middle)
    tall = jnp.concatenate([mix[:, :middle], mix[:, middle:]], axis=0)
    second = jnp.concatenate([conv[:, 2], tall], axis=1)
    return first, second


def unpack(total, middle):
    rows = total.shape[0] // 2
    leading = lax.axis_index("dp") == 0
    got = cross(jnp.where(leading, total[rows:], total[:rows]))
    first = jnp.where(leading, total[:rows], got)
    second = jnp.where(leading, got, total[rows:])
    conv = jnp.concatenate(
        [first.reshape(rows, 2, middle), second[:, None, :middle]], axis=1
    )
    half = rows // 2
    mix = jnp.concatenate([second[:half, middle:], second[half:, middle:]], axis=1)
    return conv, mix


def body(activations, cotangent, conv_one, mix_one, conv_two, mix_two):
    count = lax.axis_size("seq")
    orders = step_orders(count)
    depth = len(orders[0])
    middle = conv_one.shape[2]
    length = activations.shape[1]
    leading = lax.axis_index("dp") == 0

    packed = [pack(conv_one, mix_one), pack(conv_two, mix_two)]
    mine = [jnp.where(leading, first, second) for first, second in packed]
    got = cross(jnp.stack([jnp.where(leading, second, first) for first, second in packed]))
    own_one, own_two = (
        jnp.where(
            leading,
            jnp.concatenate([mine[b], got[b]], axis=0),
            jnp.concatenate([got[b], mine[b]], axis=0),
        )[None]
        for b in range(2)
    )
    low, high = halo(
        activations[:, :DILATE_ONE], activations[:, length - DILATE_ONE :]
    )
    own_one = widen(own_one, orders, 0)
    ext_one = norm_ext(activations, low, high)
    own_one, own_two, ext_one = tie(own_one, own_two, ext_one)
    for j in range(1, depth):
        own_one, own_two = tie(widen(own_one, orders, j), widen(own_two, orders, j - 1))
    pieces_one = (own_one, cross(own_one))
    own_two = widen(own_two, orders, depth - 1)
    pre_one, hid_one, second_in, first, last = forward_block(
        ext_one, activations, pieces_one, orders, DILATE_ONE, DILATE_TWO
    )
    own_two, first, last = tie(own_two, first, last)
    low, high = halo(first, last)
    pieces_two = (own_two, cross(own_two))
    ext_two, hid_two, dpre_two, dfirst, dlast = turn_block(
        first, last, low, high, cotangent, pieces_two, orders, DILATE_TWO
    )
    dlow, dhigh = halo(dfirst, dlast)
    keep, send = grads_block(ext_two, hid_two, cotangent, dpre_two, orders, DILATE_TWO, count)
    dlow, dhigh, keep, send = tie(dlow, dhigh, keep, send)
    total_two = keep + cross(send).astype(F32)
    total_two, dlow, dhigh = tie(total_two, dlow, dhigh)
    upstream, dpre_one, dfirst, dlast = back_block(
        dpre_two, dlow, dhigh, second_in, cotangent, pieces_two, orders, DILATE_TWO,
        (pieces_one, pre_one, DILATE_ONE),
    )
    dlow, dhigh = halo(dfirst, dlast)
    keep, send = grads_block(ext_one, hid_one, upstream, dpre_one, orders, DILATE_ONE, count)
    total_two = fold(total_two, orders, depth - 1)
    total_two, keep, send, dlow, dhigh = tie(total_two, keep, send, dlow, dhigh)
    total_one = keep + cross(send).astype(F32)
    (input_grad,) = back_block(
        dpre_one, dlow, dhigh, activations, upstream, pieces_one, orders, DILATE_ONE
    )
    for j in reversed(range(depth - 1)):
        total_two = fold(total_two, orders, j)
    for j in reversed(range(depth)):
        total_one = fold(total_one, orders, j)
    return (input_grad, *unpack(total_one[0], middle), *unpack(total_two[0], middle))


def solution(mesh):
    in_specs = (
        P(("parts", "dp"), "seq", None),
        P(("parts", "dp"), "seq", None),
        P(("seq", "dp"), None, None),
        P(("seq", "dp"), None),
        P(("seq", "dp"), None, None),
        P(("seq", "dp"), None),
    )
    out_specs = (
        P(("parts", "dp"), "seq", None),
        P(("parts", "seq", "dp"), None, None),
        P(("parts", "seq", "dp"), None),
        P(("parts", "seq", "dp"), None, None),
        P(("parts", "seq", "dp"), None),
    )
    return jax.shard_map(body, mesh=mesh, in_specs=in_specs, out_specs=out_specs, check_vma=False)
```

```python
import functools
import math

import jax
import jax.numpy as jnp
from jax import lax
from jax.experimental import pallas as pl
from jax.experimental.pallas import tpu as pltpu
from jax.sharding import PartitionSpec as P

DILATE_ONE = 64
DILATE_TWO = 128
BF = jnp.bfloat16
F32 = jnp.float32
ROOT = math.sqrt(2.0 / math.pi)
CUBE = 0.044715
VMEM = pl.BlockSpec(memory_space=pltpu.VMEM)
NT = (((1,), (1,)), ((), ()))
TN = (((0,), (0,)), ((), ()))


def gelu(v):
    return v * (0.5 * (1.0 + jnp.tanh(ROOT * (v + CUBE * (v * v * v)))))


def gelu_slope(v):
    t = jnp.tanh(ROOT * (v + CUBE * (v * v * v)))
    return 0.5 * (1.0 + t) + (0.5 * v) * (1.0 - t * t) * (ROOT * (1.0 + 3.0 * CUBE * (v * v)))


def norm_scale(v):
    return lax.rsqrt(jnp.mean(v * v, axis=-1, keepdims=True) + 1e-06)


def dot(a, b, dims=(((1,), (0,)), ((), ()))):
    return lax.dot_general(a, b, dims, preferred_element_type=F32)


def cost(flat, width, middle):
    return pl.CostEstimate(
        flops=8 * flat * width * middle, bytes_accessed=8 << 20, transcendentals=0
    )


def params():
    return pltpu.CompilerParams(vmem_limit_bytes=16 << 20)


def tie(*values):
    return lax.optimization_barrier(values)


def step_orders(count):
    bits = [1 << i for i in reversed(range(count.bit_length() - 1))]
    assert math.prod([2] * len(bits)) == count
    return bits, bits[-1:] + bits[:-1]


def place_of(offset, steps):
    place = 0
    for j, step in enumerate(steps):
        shift = step.bit_length() - 1
        place = place + (((offset >> shift) & 1) << j)
    return place


def cross(value):
    return lax.ppermute(value, "dp", [(0, 1), (1, 0)])


def hop(value, orders, j):
    count = lax.axis_size("seq")
    pairs = [
        (2 * i + core, 2 * (i ^ orders[core][j]) + core)
        for i in range(count)
        for core in range(2)
    ]
    return lax.ppermute(value, ("seq", "dp"), pairs)


def widen(value, got):
    return jnp.concatenate([value, got], axis=0)


def give(total, orders, j):
    return hop(total[total.shape[0] // 2 :].astype(BF), orders, j)


def fold_all(keep, got):
    return keep + got.astype(F32)


def fold(total, got):
    return total[: total.shape[0] // 2] + got.astype(F32)


def halo(first, last):
    count = lax.axis_size("seq")
    low = lax.ppermute(last, "seq", [(i, i + 2) for i in range(count - 2)])
    high = lax.ppermute(first, "seq", [(i + 2, i) for i in range(count - 2)])
    return low, high


def swap_pair(value):
    count = lax.axis_size("seq")
    return lax.ppermute(value, "seq", [(i, i ^ 1) for i in range(count)])


def ordered(leading, mine, theirs):
    return jnp.concatenate(
        [jnp.where(leading, mine, theirs), jnp.where(leading, theirs, mine)], axis=0
    )


def split_pair(field, axis):
    even = lax.axis_index("seq") % 2 == 0
    half = field.shape[axis] // 2
    low = lax.slice_in_dim(field, 0, half, axis=axis)
    high = lax.slice_in_dim(field, half, 2 * half, axis=axis)
    return jnp.where(even, low, high), jnp.where(even, high, low)


def join_pair(mine, theirs, axis):
    even = lax.axis_index("seq") % 2 == 0
    return jnp.concatenate(
        [jnp.where(even, mine, theirs), jnp.where(even, theirs, mine)], axis=axis
    )


def with_weights(pieces, orders, middle, run):
    here, core = lax.axis_index("seq"), lax.axis_index("dp")
    own, other = pieces
    count, rows = own.shape[:2]
    part = rows // 4

    def case(taps, rest):
        def whole(ref, steps, half):
            cols = slice(half * middle, (half + 1) * middle)
            return jnp.concatenate(
                [ref[place_of(here ^ chip, steps), :, cols] for chip in range(count)], axis=0
            )

        def mix(h):
            pieces = []
            for chip in range(count):
                place = place_of(here ^ chip, orders[1])
                for lane in range(2):
                    start = (2 * lane + h) * part
                    pieces.append(rest[place, start : start + part, middle:])
            return jnp.concatenate(pieces, axis=0)

        run(
            [
                lambda: whole(taps, orders[0], 0),
                lambda: whole(taps, orders[0], 1),
                lambda: whole(rest, orders[1], 0),
            ],
            [lambda: mix(0), lambda: mix(1)],
        )

    @pl.when(core == 0)
    def _():
        case(own, other)

    @pl.when(core == 1)
    def _():
        case(other, own)


def norm_rows(source, w, start, size, target, put):
    @pl.loop(0, size // 32)
    def _(i):
        rows = pl.multiple_of(i * 32, 32)
        v = source[w, pl.ds(start + rows, 32), :].astype(F32)
        target[w, pl.ds(put + rows, 32), :] = gelu(v * norm_scale(v)).astype(BF)


def norm_kernel(x_ref, low_ref, high_ref, ext_ref):
    dilate = low_ref.shape[1]
    length = x_ref.shape[1]
    for w in range(x_ref.shape[0]):
        norm_rows(low_ref, w, 0, dilate, ext_ref, 0)
        norm_rows(x_ref, w, 0, length, ext_ref, dilate)
        norm_rows(high_ref, w, 0, dilate, ext_ref, dilate + length)


def norm_ext(x, low, high):
    windows, length, width = x.shape
    return pl.pallas_call(
        norm_kernel,
        out_shape=jax.ShapeDtypeStruct((windows, length + 2 * low.shape[1], width), BF),
        in_specs=[VMEM] * 3,
        out_specs=VMEM,
        compiler_params=params(),
        name="norm_ext",
    )(x, low, high)


def forward_kernel(
    orders, dilate, edge, ext, x_ref, own, other, pre_ref, hid_ref, x2_ref, first_ref, last_ref
):
    pieces = (own, other)
    windows, length, width = x_ref.shape
    middle = hid_ref.shape[1]

    def run(conv, mix):
        for w in range(windows):
            rows = slice(w * length, (w + 1) * length)
            pre = sum(dot(ext[w, k * dilate : k * dilate + length, :], conv[k]()) for k in range(3))
            pre_ref[rows, :] = pre
            hid = gelu(pre).astype(BF)
            hid_ref[rows, :] = hid
            for h in range(2):
                cols = slice(h * middle, (h + 1) * middle)
                x2_ref[w, :, cols] = (x_ref[w, :, cols].astype(F32) + dot(hid, mix[h]())).astype(BF)

    with_weights(pieces, orders, middle, run)
    for w in range(windows):
        norm_rows(x2_ref, w, 0, edge, first_ref, 0)
        norm_rows(x2_ref, w, length - edge, edge, last_ref, 0)


def forward_block(ext, x, pieces, orders, dilate, edge):
    windows, length, width = x.shape
    middle = pieces[0].shape[2] // 2
    flat = windows * length
    return pl.pallas_call(
        functools.partial(forward_kernel, orders, dilate, edge),
        out_shape=(
            jax.ShapeDtypeStruct((flat, middle), F32),
            jax.ShapeDtypeStruct((flat, middle), BF),
            jax.ShapeDtypeStruct(x.shape, BF),
            jax.ShapeDtypeStruct((windows, edge, width), BF),
            jax.ShapeDtypeStruct((windows, edge, width), BF),
        ),
        in_specs=[VMEM] * 4,
        out_specs=(VMEM,) * 5,
        compiler_params=params(),
        cost_estimate=cost(flat, width, middle),
        name="forward_block",
    )(ext, x, *pieces)


def turn_kernel(
    orders, dilate, first, last, low, high, x_ref, e_ref, own, other,
    ext, hid_ref, dpre_ref, dfirst, dlast,
):
    pieces = (own, other)
    windows, length, width = e_ref.shape
    edge = first.shape[1]
    middle = hid_ref.shape[1]
    for w in range(windows):
        for source, start in (
            (low, 0), (first, dilate), (last, dilate + length - edge), (high, dilate + length),
        ):
            ext[w, start : start + edge, :] = source[w]
        norm_rows(x_ref, w, edge, length - 2 * edge, ext, dilate + edge)

    def run(conv, mix):
        for w in range(windows):
            rows = slice(w * length, (w + 1) * length)
            pre = sum(dot(ext[w, k * dilate : k * dilate + length, :], conv[k]()) for k in range(3))
            dhid = dot(e_ref[w, :, :middle], mix[0](), NT) + dot(e_ref[w, :, middle:], mix[1](), NT)
            hid_ref[rows, :] = gelu(pre).astype(BF)
            dpre_ref[rows, :] = (gelu_slope(pre) * dhid).astype(BF)

    with_weights(pieces, orders, middle, run)
    for w in range(windows):
        dfirst[w] = dpre_ref[w * length : w * length + dilate, :]
        dlast[w] = dpre_ref[(w + 1) * length - dilate : (w + 1) * length, :]


def turn_block(first, last, low, high, x, e, pieces, orders, dilate):
    windows, length, width = e.shape
    middle = pieces[0].shape[2] // 2
    flat = windows * length
    return pl.pallas_call(
        functools.partial(turn_kernel, orders, dilate),
        out_shape=(
            jax.ShapeDtypeStruct((windows, length + 2 * dilate, width), BF),
            jax.ShapeDtypeStruct((flat, middle), BF),
            jax.ShapeDtypeStruct((flat, middle), BF),
            jax.ShapeDtypeStruct((windows, dilate, middle), BF),
            jax.ShapeDtypeStruct((windows, dilate, middle), BF),
        ),
        in_specs=[VMEM] * 8,
        out_specs=(VMEM,) * 5,
        compiler_params=params(),
        cost_estimate=cost(flat, width, middle),
        name="turn_block",
    )(first, last, low, high, x, e, *pieces)


def grads_kernel(orders, dilate, ext, hid, e_ref, dpre, keep, send, full):
    here, core = lax.axis_index("seq"), lax.axis_index("dp")
    windows, length, width = e_ref.shape
    middle = hid.shape[1]
    count, rows = keep.shape[:2]
    part = rows // 4

    def put(target, k):
        steps = orders[k // 2]
        cols = slice((k % 2) * middle, (k % 2 + 1) * middle)
        for chip in range(count):
            place = place_of(here ^ chip, steps)
            if k < 3:
                value = full[chip * rows : (chip + 1) * rows, :]
                target[place, :, cols] = value.astype(target.dtype)
                continue
            for lane in range(2):
                for h in range(2):
                    base = h * middle + (2 * chip + lane) * part
                    start = (2 * lane + h) * part
                    value = full[base : base + part, :]
                    target[place, start : start + part, cols] = value.astype(target.dtype)

    for k in range(4):
        if k == 3:
            for h in range(2):
                e = jnp.concatenate(
                    [e_ref[w, :, h * middle : (h + 1) * middle] for w in range(windows)], axis=0
                )
                full[h * middle : (h + 1) * middle, :] = dot(hid[...], e, TN)
        else:
            view = jnp.concatenate(
                [ext[w, k * dilate : k * dilate + length, :] for w in range(windows)], axis=0
            )
            full[...] = dot(view, dpre[...], TN)

        @pl.when(core == k // 2)
        def _():
            put(keep, k)

        @pl.when(core != k // 2)
        def _():
            put(send, k)


def grads_block(ext, hid, e, dpre, orders, dilate, count):
    windows, length, width = e.shape
    flat, middle = hid.shape
    shape = (count, width // count, 2 * middle)
    return pl.pallas_call(
        functools.partial(grads_kernel, orders, dilate),
        out_shape=(jax.ShapeDtypeStruct(shape, F32), jax.ShapeDtypeStruct(shape, BF)),
        in_specs=[VMEM] * 4,
        out_specs=(VMEM,) * 2,
        scratch_shapes=[pltpu.VMEM((width, middle), F32)],
        compiler_params=params(),
        cost_estimate=cost(flat, width, middle),
        name="grads_block",
    )(ext, hid, e, dpre)


def back_kernel(orders, dilate, chained, *refs):
    dpre, low, high, x_ref, e_ref = refs[:5]
    pieces = refs[5:7]
    if chained:
        pieces_m = refs[7:9]
        pre_ref, out_ref, dprev, dfirst, dlast, ext, dn = refs[9:]
    else:
        out_ref, ext, dn = refs[7:]
    windows, length, width = x_ref.shape
    middle = dpre.shape[1]
    for w in range(windows):
        ext[w, :dilate, :] = low[w]
        ext[w, dilate : dilate + length, :] = dpre[w * length : (w + 1) * length, :]
        ext[w, dilate + length :, :] = high[w]

    def run(conv, mix):
        for w in range(windows):
            dn[w] = sum(
                dot(ext[w, (2 - k) * dilate : (2 - k) * dilate + length, :], conv[k](), NT)
                for k in range(3)
            )

    with_weights(pieces, orders, middle, run)
    for w in range(windows):

        @pl.loop(0, length // 32)
        def _(i):
            rows = pl.ds(pl.multiple_of(i * 32, 32), 32)
            v = x_ref[w, rows, :].astype(F32)
            scale = norm_scale(v)
            u = v * scale
            g = dn[w, rows, :] * gelu_slope(u)
            dv = scale * (g - u * jnp.mean(g * u, axis=-1, keepdims=True))
            out_ref[w, rows, :] = (e_ref[w, rows, :].astype(F32) + dv).astype(BF)

    if chained:

        def turn(conv, mix):
            for w in range(windows):
                dhid = dot(out_ref[w, :, :middle], mix[0](), NT) + dot(
                    out_ref[w, :, middle:], mix[1](), NT
                )
                rows = slice(w * length, (w + 1) * length)
                dprev[rows, :] = (gelu_slope(pre_ref[rows, :]) * dhid).astype(BF)

        with_weights(pieces_m, orders, middle, turn)
        edge = dfirst.shape[1]
        for w in range(windows):
            dfirst[w] = dprev[w * length : w * length + edge, :]
            dlast[w] = dprev[(w + 1) * length - edge : (w + 1) * length, :]


def back_block(dpre, low, high, x, e, pieces, orders, dilate, previous=None):
    windows, length, width = x.shape
    flat, middle = dpre.shape
    chained = previous is not None
    operands = [dpre, low, high, x, e, *pieces]
    shapes = [jax.ShapeDtypeStruct(x.shape, BF)]
    if chained:
        others, pre, edge = previous
        operands += [*others, pre]
        shapes += [
            jax.ShapeDtypeStruct((flat, middle), BF),
            jax.ShapeDtypeStruct((windows, edge, middle), BF),
            jax.ShapeDtypeStruct((windows, edge, middle), BF),
        ]
    return pl.pallas_call(
        functools.partial(back_kernel, orders, dilate, chained),
        out_shape=tuple(shapes),
        in_specs=[VMEM] * len(operands),
        out_specs=(VMEM,) * len(shapes),
        scratch_shapes=[
            pltpu.VMEM((windows, length + 2 * dilate, middle), BF),
            pltpu.VMEM((windows, length, width), F32),
        ],
        compiler_params=params(),
        cost_estimate=cost(flat, width, middle),
        name="back_block",
    )(*operands)


def pack(conv, mix):
    middle = conv.shape[2]
    first = conv[:, :2].reshape(conv.shape[0], 2 * middle)
    tall = jnp.concatenate([mix[:, :middle], mix[:, middle:]], axis=0)
    second = jnp.concatenate([conv[:, 2], tall], axis=1)
    return first, second


def unpack(total, middle):
    rows = total.shape[0] // 2
    leading = lax.axis_index("dp") == 0
    got = cross(jnp.where(leading, total[rows:], total[:rows]))
    first = jnp.where(leading, total[:rows], got)
    second = jnp.where(leading, got, total[rows:])
    conv = jnp.concatenate(
        [first.reshape(rows, 2, middle), second[:, None, :middle]], axis=1
    )
    half = rows // 2
    mix = jnp.concatenate([second[:half, middle:], second[half:, middle:]], axis=1)
    return conv, mix


def body(activations, cotangent, conv_one, mix_one, conv_two, mix_two):
    count = lax.axis_size("seq")
    orders = step_orders(count)
    last_step = len(orders[0]) - 1
    middle = conv_one.shape[2]
    leading = lax.axis_index("dp") == 0

    def chip_part(conv, mix):
        first, second = pack(conv, mix)
        got = cross(jnp.where(leading, second, first))
        return ordered(leading, jnp.where(leading, first, second), got)[None]

    own_one = chip_part(conv_one, mix_one)
    got_one = hop(own_one, orders, 0)
    activations, conv_two, mix_two, own_one = tie(activations, conv_two, mix_two, own_one)
    mine_x, gives_x = split_pair(activations, 0)
    got_x = swap_pair(gives_x)
    own_two = chip_part(conv_two, mix_two)
    own_one = widen(own_one, got_one)
    got_one = hop(own_one, orders, 1)
    got_two = hop(own_two, orders, 0)
    own_one, cotangent, got_x = tie(own_one, cotangent, got_x)
    x = join_pair(mine_x, got_x, 1)
    length = x.shape[1]
    low, high = halo(x[:, :DILATE_ONE], x[:, length - DILATE_ONE :])
    mine_e, gives_e = split_pair(cotangent, 0)
    got_e = swap_pair(gives_e)
    ext_one = norm_ext(x, low, high)
    got_one, got_two, ext_one = tie(got_one, got_two, ext_one)
    for j in range(2, last_step + 1):
        own_one, own_two = widen(own_one, got_one), widen(own_two, got_two)
        got_one, got_two = tie(hop(own_one, orders, j), hop(own_two, orders, j - 1))
    own_one = widen(own_one, got_one)
    got_one = cross(own_one)
    own_one, got_two = tie(own_one, got_two)
    own_two = widen(own_two, got_two)
    got_two = hop(own_two, orders, last_step)
    e = join_pair(mine_e, got_e, 1)
    pieces_one = (own_one, got_one)
    pre_one, hid_one, second_in, first, last = forward_block(
        ext_one, x, pieces_one, orders, DILATE_ONE, DILATE_TWO
    )
    low, high = halo(first, last)
    got_two, first, last = tie(got_two, first, last)
    own_two = widen(own_two, got_two)
    pieces_two = (own_two, cross(own_two))
    ext_two, hid_two, dpre_two, dfirst, dlast = turn_block(
        first, last, low, high, second_in, e, pieces_two, orders, DILATE_TWO
    )

    dlow, dhigh = halo(dfirst, dlast)
    keep_two, send = grads_block(ext_two, hid_two, e, dpre_two, orders, DILATE_TWO, count)
    dlow, dhigh, send = tie(dlow, dhigh, send)
    got_two = cross(send)
    upstream, dpre_one, dfirst, dlast = back_block(
        dpre_two, dlow, dhigh, second_in, e, pieces_two, orders, DILATE_TWO,
        (pieces_one, pre_one, DILATE_ONE),
    )
    got_two, dpre_one, upstream = tie(got_two, dpre_one, upstream)
    total_two = fold_all(keep_two, got_two)
    got_two = give(total_two, orders, last_step)
    total_two, dpre_one = tie(total_two, dpre_one)
    keep_one, send = grads_block(ext_one, hid_one, upstream, dpre_one, orders, DILATE_ONE, count)
    got_one = cross(send)
    dfirst, dlast, send, got_two = tie(dfirst, dlast, send, got_two)
    dlow, dhigh = halo(dfirst, dlast)
    total_one = fold_all(keep_one, got_one)
    got_one = give(total_one, orders, last_step)
    total_one, dlow, dhigh, got_two = tie(total_one, dlow, dhigh, got_two)
    (input_grad,) = back_block(
        dpre_one, dlow, dhigh, x, upstream, pieces_one, orders, DILATE_ONE
    )
    input_grad, got_one, got_two = tie(input_grad, got_one, got_two)
    mine_g, gives_g = split_pair(input_grad, 1)
    for j in reversed(range(last_step)):
        total_two = fold(total_two, got_two)
        got_two = give(total_two, orders, j)
        total_one = fold(total_one, got_one)
        got_one = give(total_one, orders, j)
        if j == last_step - 1:
            total_one, gives_g = tie(total_one, gives_g)
            got_g = swap_pair(gives_g)
        if j > 0:
            got_one, got_two = tie(got_one, got_two)
    total_two = fold(total_two, got_two)
    grads_two = unpack(total_two[0], middle)
    grads_two, got_one, got_g = tie(grads_two, got_one, got_g)
    total_one = fold(total_one, got_one)
    input_grad = join_pair(mine_g, got_g, 0)
    return (input_grad, *unpack(total_one[0], middle), *grads_two)


def solution(mesh):
    in_specs = (
        P(("parts", "dp"), "seq", None),
        P(("parts", "dp"), "seq", None),
        P(("seq", "dp"), None, None),
        P(("seq", "dp"), None),
        P(("seq", "dp"), None, None),
        P(("seq", "dp"), None),
    )
    out_specs = (
        P(("parts", "dp"), "seq", None),
        P(("parts", "seq", "dp"), None, None),
        P(("parts", "seq", "dp"), None),
        P(("parts", "seq", "dp"), None, None),
        P(("parts", "seq", "dp"), None),
    )
    return jax.shard_map(body, mesh=mesh, in_specs=in_specs, out_specs=out_specs, check_vma=False)
```

```python
import functools
import math

import jax
import jax.numpy as jnp
from jax import lax
from jax.experimental import pallas as pl
from jax.experimental.pallas import tpu as pltpu
from jax.sharding import PartitionSpec as P

DILATE_ONE = 64
DILATE_TWO = 128
BF = jnp.bfloat16
F32 = jnp.float32
ROOT = math.sqrt(2.0 / math.pi)
CUBE = 0.044715
VMEM = pl.BlockSpec(memory_space=pltpu.VMEM)
NT = (((1,), (1,)), ((), ()))
TN = (((0,), (0,)), ((), ()))


def gelu(v):
    return v * (0.5 * (1.0 + jnp.tanh(ROOT * (v + CUBE * (v * v * v)))))


def gelu_slope(v):
    t = jnp.tanh(ROOT * (v + CUBE * (v * v * v)))
    return 0.5 * (1.0 + t) + (0.5 * v) * (1.0 - t * t) * (ROOT * (1.0 + 3.0 * CUBE * (v * v)))


def norm_scale(v):
    return lax.rsqrt(jnp.mean(v * v, axis=-1, keepdims=True) + 1e-06)


def dot(a, b, dims=(((1,), (0,)), ((), ()))):
    return lax.dot_general(a, b, dims, preferred_element_type=F32)


def cost(flat, width, middle):
    return pl.CostEstimate(
        flops=8 * flat * width * middle, bytes_accessed=8 << 20, transcendentals=0
    )


def params():
    return pltpu.CompilerParams(vmem_limit_bytes=16 << 20)


def tie(*values):
    return lax.optimization_barrier(values)


def step_orders(count):
    bits = [1 << i for i in reversed(range(count.bit_length() - 1))]
    assert math.prod([2] * len(bits)) == count
    return bits[:-2] + bits[:-3:-1], bits


def place_of(offset, steps):
    place = 0
    for j, step in enumerate(steps):
        shift = step.bit_length() - 1
        place = place + (((offset >> shift) & 1) << j)
    return place


def cross(value):
    return lax.ppermute(value, "dp", [(0, 1), (1, 0)])


def hop(value, orders, j):
    count = lax.axis_size("seq")
    pairs = [
        (2 * i + core, 2 * (i ^ orders[core][j]) + core)
        for i in range(count)
        for core in range(2)
    ]
    return lax.ppermute(value, ("seq", "dp"), pairs)


def widen(value, got):
    return jnp.concatenate([value, got], axis=0)


def give(total, orders, j):
    return hop(total[total.shape[0] // 2 :].astype(BF), orders, j)


def fold_all(keep, got):
    return keep + got.astype(F32)


def fold(total, got):
    return total[: total.shape[0] // 2] + got.astype(F32)


def halo(first, last):
    count = lax.axis_size("seq")
    low = lax.ppermute(last, "seq", [(i, i + 2) for i in range(count - 2)])
    high = lax.ppermute(first, "seq", [(i + 2, i) for i in range(count - 2)])
    return low, high


def swap_pair(value):
    count = lax.axis_size("seq")
    return lax.ppermute(value, "seq", [(i, i ^ 1) for i in range(count)])


def ordered(leading, mine, theirs):
    return jnp.concatenate(
        [jnp.where(leading, mine, theirs), jnp.where(leading, theirs, mine)], axis=0
    )


def split_pair(field, axis):
    even = lax.axis_index("seq") % 2 == 0
    half = field.shape[axis] // 2
    low = lax.slice_in_dim(field, 0, half, axis=axis)
    high = lax.slice_in_dim(field, half, 2 * half, axis=axis)
    return jnp.where(even, low, high), jnp.where(even, high, low)


def join_pair(mine, theirs, axis):
    even = lax.axis_index("seq") % 2 == 0
    return jnp.concatenate(
        [jnp.where(even, mine, theirs), jnp.where(even, theirs, mine)], axis=axis
    )


def with_weights(pieces, orders, middle, run):
    here, core = lax.axis_index("seq"), lax.axis_index("dp")
    own, other = pieces
    count, rows = own.shape[:2]
    part = rows // 4

    def case(taps, rest):
        def whole(ref, steps, half):
            cols = slice(half * middle, (half + 1) * middle)
            return jnp.concatenate(
                [ref[place_of(here ^ chip, steps), :, cols] for chip in range(count)], axis=0
            )

        def mix(h):
            pieces = []
            for chip in range(count):
                place = place_of(here ^ chip, orders[1])
                for lane in range(2):
                    start = (2 * lane + h) * part
                    pieces.append(rest[place, start : start + part, middle:])
            return jnp.concatenate(pieces, axis=0)

        run(
            [
                lambda: whole(taps, orders[0], 0),
                lambda: whole(taps, orders[0], 1),
                lambda: whole(rest, orders[1], 0),
            ],
            [lambda: mix(0), lambda: mix(1)],
        )

    @pl.when(core == 0)
    def _():
        case(own, other)

    @pl.when(core == 1)
    def _():
        case(other, own)


def norm_rows(source, w, start, size, target, put):
    @pl.loop(0, size // 32)
    def _(i):
        rows = pl.multiple_of(i * 32, 32)
        v = source[w, pl.ds(start + rows, 32), :].astype(F32)
        target[w, pl.ds(put + rows, 32), :] = gelu(v * norm_scale(v)).astype(BF)


def norm_kernel(x_ref, low_ref, high_ref, ext_ref):
    dilate = low_ref.shape[1]
    length = x_ref.shape[1]
    for w in range(x_ref.shape[0]):
        norm_rows(low_ref, w, 0, dilate, ext_ref, 0)
        norm_rows(x_ref, w, 0, length, ext_ref, dilate)
        norm_rows(high_ref, w, 0, dilate, ext_ref, dilate + length)


def norm_ext(x, low, high):
    windows, length, width = x.shape
    return pl.pallas_call(
        norm_kernel,
        out_shape=jax.ShapeDtypeStruct((windows, length + 2 * low.shape[1], width), BF),
        in_specs=[VMEM] * 3,
        out_specs=VMEM,
        compiler_params=params(),
        name="norm_ext",
    )(x, low, high)


def forward_kernel(
    orders, dilate, edge, ext, x_ref, own, other, pre_ref, hid_ref, x2_ref, first_ref, last_ref
):
    pieces = (own, other)
    windows, length, width = x_ref.shape
    middle = hid_ref.shape[1]

    def run(conv, mix):
        for w in range(windows):
            rows = slice(w * length, (w + 1) * length)
            pre = sum(dot(ext[w, k * dilate : k * dilate + length, :], conv[k]()) for k in range(3))
            pre_ref[rows, :] = pre
            hid = gelu(pre).astype(BF)
            hid_ref[rows, :] = hid
            for h in range(2):
                cols = slice(h * middle, (h + 1) * middle)
                x2_ref[w, :, cols] = (x_ref[w, :, cols].astype(F32) + dot(hid, mix[h]())).astype(BF)

    with_weights(pieces, orders, middle, run)
    for w in range(windows):
        norm_rows(x2_ref, w, 0, edge, first_ref, 0)
        norm_rows(x2_ref, w, length - edge, edge, last_ref, 0)


def forward_block(ext, x, pieces, orders, dilate, edge):
    windows, length, width = x.shape
    middle = pieces[0].shape[2] // 2
    flat = windows * length
    return pl.pallas_call(
        functools.partial(forward_kernel, orders, dilate, edge),
        out_shape=(
            jax.ShapeDtypeStruct((flat, middle), F32),
            jax.ShapeDtypeStruct((flat, middle), BF),
            jax.ShapeDtypeStruct(x.shape, BF),
            jax.ShapeDtypeStruct((windows, edge, width), BF),
            jax.ShapeDtypeStruct((windows, edge, width), BF),
        ),
        in_specs=[VMEM] * 4,
        out_specs=(VMEM,) * 5,
        compiler_params=params(),
        cost_estimate=cost(flat, width, middle),
        name="forward_block",
    )(ext, x, *pieces)


def turn_kernel(
    orders, dilate, first, last, low, high, x_ref, e_ref, own, other,
    ext, hid_ref, dpre_ref, dfirst, dlast,
):
    pieces = (own, other)
    windows, length, width = e_ref.shape
    edge = first.shape[1]
    middle = hid_ref.shape[1]
    for w in range(windows):
        for source, start in (
            (low, 0), (first, dilate), (last, dilate + length - edge), (high, dilate + length),
        ):
            ext[w, start : start + edge, :] = source[w]
        norm_rows(x_ref, w, edge, length - 2 * edge, ext, dilate + edge)

    def run(conv, mix):
        for w in range(windows):
            rows = slice(w * length, (w + 1) * length)
            pre = sum(dot(ext[w, k * dilate : k * dilate + length, :], conv[k]()) for k in range(3))
            dhid = dot(e_ref[w, :, :middle], mix[0](), NT) + dot(e_ref[w, :, middle:], mix[1](), NT)
            hid_ref[rows, :] = gelu(pre).astype(BF)
            dpre_ref[rows, :] = (gelu_slope(pre) * dhid).astype(BF)

    with_weights(pieces, orders, middle, run)
    for w in range(windows):
        dfirst[w] = dpre_ref[w * length : w * length + dilate, :]
        dlast[w] = dpre_ref[(w + 1) * length - dilate : (w + 1) * length, :]


def turn_block(first, last, low, high, x, e, pieces, orders, dilate):
    windows, length, width = e.shape
    middle = pieces[0].shape[2] // 2
    flat = windows * length
    return pl.pallas_call(
        functools.partial(turn_kernel, orders, dilate),
        out_shape=(
            jax.ShapeDtypeStruct((windows, length + 2 * dilate, width), BF),
            jax.ShapeDtypeStruct((flat, middle), BF),
            jax.ShapeDtypeStruct((flat, middle), BF),
            jax.ShapeDtypeStruct((windows, dilate, middle), BF),
            jax.ShapeDtypeStruct((windows, dilate, middle), BF),
        ),
        in_specs=[VMEM] * 8,
        out_specs=(VMEM,) * 5,
        compiler_params=params(),
        cost_estimate=cost(flat, width, middle),
        name="turn_block",
    )(first, last, low, high, x, e, *pieces)


def grads_kernel(orders, dilate, ext, hid, e_ref, dpre, keep, send, full):
    here, core = lax.axis_index("seq"), lax.axis_index("dp")
    windows, length, width = e_ref.shape
    middle = hid.shape[1]
    count, rows = keep.shape[:2]
    part = rows // 4

    def put(target, k):
        steps = orders[k // 2]
        cols = slice((k % 2) * middle, (k % 2 + 1) * middle)
        for chip in range(count):
            place = place_of(here ^ chip, steps)
            if k < 3:
                value = full[chip * rows : (chip + 1) * rows, :]
                target[place, :, cols] = value.astype(target.dtype)
                continue
            for lane in range(2):
                for h in range(2):
                    base = h * middle + (2 * chip + lane) * part
                    start = (2 * lane + h) * part
                    value = full[base : base + part, :]
                    target[place, start : start + part, cols] = value.astype(target.dtype)

    for k in range(4):
        if k == 3:
            for h in range(2):
                e = jnp.concatenate(
                    [e_ref[w, :, h * middle : (h + 1) * middle] for w in range(windows)], axis=0
                )
                full[h * middle : (h + 1) * middle, :] = dot(hid[...], e, TN)
        else:
            view = jnp.concatenate(
                [ext[w, k * dilate : k * dilate + length, :] for w in range(windows)], axis=0
            )
            full[...] = dot(view, dpre[...], TN)

        @pl.when(core == k // 2)
        def _():
            put(keep, k)

        @pl.when(core != k // 2)
        def _():
            put(send, k)


def grads_block(ext, hid, e, dpre, orders, dilate, count):
    windows, length, width = e.shape
    flat, middle = hid.shape
    shape = (count, width // count, 2 * middle)
    return pl.pallas_call(
        functools.partial(grads_kernel, orders, dilate),
        out_shape=(jax.ShapeDtypeStruct(shape, F32), jax.ShapeDtypeStruct(shape, BF)),
        in_specs=[VMEM] * 4,
        out_specs=(VMEM,) * 2,
        scratch_shapes=[pltpu.VMEM((width, middle), F32)],
        compiler_params=params(),
        cost_estimate=cost(flat, width, middle),
        name="grads_block",
    )(ext, hid, e, dpre)


def back_kernel(orders, dilate, chained, *refs):
    dpre, low, high, x_ref, e_ref = refs[:5]
    pieces = refs[5:7]
    if chained:
        pieces_m = refs[7:9]
        pre_ref, out_ref, dprev, dfirst, dlast, ext, dn = refs[9:]
    else:
        out_ref, ext, dn = refs[7:]
    windows, length, width = x_ref.shape
    middle = dpre.shape[1]
    for w in range(windows):
        ext[w, :dilate, :] = low[w]
        ext[w, dilate : dilate + length, :] = dpre[w * length : (w + 1) * length, :]
        ext[w, dilate + length :, :] = high[w]

    def run(conv, mix):
        for w in range(windows):
            dn[w] = sum(
                dot(ext[w, (2 - k) * dilate : (2 - k) * dilate + length, :], conv[k](), NT)
                for k in range(3)
            )

    with_weights(pieces, orders, middle, run)
    for w in range(windows):

        @pl.loop(0, length // 32)
        def _(i):
            rows = pl.ds(pl.multiple_of(i * 32, 32), 32)
            v = x_ref[w, rows, :].astype(F32)
            scale = norm_scale(v)
            u = v * scale
            g = dn[w, rows, :] * gelu_slope(u)
            dv = scale * (g - u * jnp.mean(g * u, axis=-1, keepdims=True))
            out_ref[w, rows, :] = (e_ref[w, rows, :].astype(F32) + dv).astype(BF)

    if chained:

        def turn(conv, mix):
            for w in range(windows):
                dhid = dot(out_ref[w, :, :middle], mix[0](), NT) + dot(
                    out_ref[w, :, middle:], mix[1](), NT
                )
                rows = slice(w * length, (w + 1) * length)
                dprev[rows, :] = (gelu_slope(pre_ref[rows, :]) * dhid).astype(BF)

        with_weights(pieces_m, orders, middle, turn)
        edge = dfirst.shape[1]
        for w in range(windows):
            dfirst[w] = dprev[w * length : w * length + edge, :]
            dlast[w] = dprev[(w + 1) * length - edge : (w + 1) * length, :]


def back_block(dpre, low, high, x, e, pieces, orders, dilate, previous=None):
    windows, length, width = x.shape
    flat, middle = dpre.shape
    chained = previous is not None
    operands = [dpre, low, high, x, e, *pieces]
    shapes = [jax.ShapeDtypeStruct(x.shape, BF)]
    if chained:
        others, pre, edge = previous
        operands += [*others, pre]
        shapes += [
            jax.ShapeDtypeStruct((flat, middle), BF),
            jax.ShapeDtypeStruct((windows, edge, middle), BF),
            jax.ShapeDtypeStruct((windows, edge, middle), BF),
        ]
    return pl.pallas_call(
        functools.partial(back_kernel, orders, dilate, chained),
        out_shape=tuple(shapes),
        in_specs=[VMEM] * len(operands),
        out_specs=(VMEM,) * len(shapes),
        scratch_shapes=[
            pltpu.VMEM((windows, length + 2 * dilate, middle), BF),
            pltpu.VMEM((windows, length, width), F32),
        ],
        compiler_params=params(),
        cost_estimate=cost(flat, width, middle),
        name="back_block",
    )(*operands)


def pack(conv, mix):
    middle = conv.shape[2]
    first = conv[:, :2].reshape(conv.shape[0], 2 * middle)
    tall = jnp.concatenate([mix[:, :middle], mix[:, middle:]], axis=0)
    second = jnp.concatenate([conv[:, 2], tall], axis=1)
    return first, second


def unpack(total, middle):
    rows = total.shape[0] // 2
    leading = lax.axis_index("dp") == 0
    got = cross(jnp.where(leading, total[rows:], total[:rows]))
    first = jnp.where(leading, total[:rows], got)
    second = jnp.where(leading, got, total[rows:])
    conv = jnp.concatenate(
        [first.reshape(rows, 2, middle), second[:, None, :middle]], axis=1
    )
    half = rows // 2
    mix = jnp.concatenate([second[:half, middle:], second[half:, middle:]], axis=1)
    return conv, mix


def body(activations, cotangent, conv_one, mix_one, conv_two, mix_two):
    count = lax.axis_size("seq")
    orders = step_orders(count)
    sum_orders = orders
    last_step = len(orders[0]) - 1
    middle = conv_one.shape[2]
    leading = lax.axis_index("dp") == 0

    def chip_part(conv, mix):
        first, second = pack(conv, mix)
        got = cross(jnp.where(leading, second, first))
        return ordered(leading, jnp.where(leading, first, second), got)[None]

    own_one = chip_part(conv_one, mix_one)
    got_one = hop(own_one, orders, 0)
    activations, conv_two, mix_two, own_one = tie(activations, conv_two, mix_two, own_one)
    mine_x, gives_x = split_pair(activations, 0)
    got_x = swap_pair(gives_x)
    own_two = chip_part(conv_two, mix_two)
    own_one = widen(own_one, got_one)
    got_one = hop(own_one, orders, 1)
    got_two = hop(own_two, orders, 0)
    own_one, cotangent, got_x = tie(own_one, cotangent, got_x)
    x = join_pair(mine_x, got_x, 1)
    length = x.shape[1]
    low, high = halo(x[:, :DILATE_ONE], x[:, length - DILATE_ONE :])
    mine_e, gives_e = split_pair(cotangent, 0)
    got_e = swap_pair(gives_e)
    got_one, got_two = tie(got_one, got_two)
    for j in range(2, last_step + 1):
        own_one, own_two = widen(own_one, got_one), widen(own_two, got_two)
        got_one, got_two = hop(own_one, orders, j), hop(own_two, orders, j - 1)
        if j == last_step:
            ext_one = norm_ext(x, low, high)
            e = join_pair(mine_e, got_e, 1)
            ext_one, e, got_one, got_two = tie(ext_one, e, got_one, got_two)
        got_one, got_two = tie(got_one, got_two)
    own_one = widen(own_one, got_one)
    got_one = cross(own_one)
    own_one, got_two = tie(own_one, got_two)
    own_two = widen(own_two, got_two)
    got_two = hop(own_two, orders, last_step)
    pieces_one = (own_one, got_one)
    pre_one, hid_one, second_in, first, last = forward_block(
        ext_one, x, pieces_one, orders, DILATE_ONE, DILATE_TWO
    )
    low, high = halo(first, last)
    got_two, low, high = tie(got_two, low, high)
    own_two = widen(own_two, got_two)
    pieces_two = (own_two, cross(own_two))
    ext_two, hid_two, dpre_two, dfirst, dlast = turn_block(
        first, last, low, high, second_in, e, pieces_two, orders, DILATE_TWO
    )

    dlow, dhigh = halo(dfirst, dlast)
    keep_two, send = grads_block(
        ext_two, hid_two, e, dpre_two, sum_orders, DILATE_TWO, count
    )
    dlow, dhigh, send = tie(dlow, dhigh, send)
    got_two = cross(send)
    total_two = fold_all(keep_two, got_two)
    total_two, dlow, dhigh = tie(total_two, dlow, dhigh)
    got_two = give(total_two, sum_orders, last_step)
    upstream, dpre_one, dfirst, dlast = back_block(
        dpre_two, dlow, dhigh, second_in, e, pieces_two, orders, DILATE_TWO,
        (pieces_one, pre_one, DILATE_ONE),
    )
    keep_one, send = grads_block(ext_one, hid_one, upstream, dpre_one, orders, DILATE_ONE, count)
    got_two, send, dfirst, dlast = tie(got_two, send, dfirst, dlast)
    got_one = cross(send)
    dlow, dhigh = halo(dfirst, dlast)
    total_two = fold(total_two, got_two)
    got_two = give(total_two, sum_orders, last_step - 1)
    total_one = fold_all(keep_one, got_one)
    total_one, total_two, dlow, dhigh = tie(total_one, total_two, dlow, dhigh)
    got_one = give(total_one, orders, last_step)
    (input_grad,) = back_block(
        dpre_one, dlow, dhigh, x, upstream, pieces_one, orders, DILATE_ONE
    )
    input_grad, got_one, got_two = tie(input_grad, got_one, got_two)
    mine_g, gives_g = split_pair(input_grad, 1)
    for j in reversed(range(last_step)):
        if j < last_step - 1:
            total_two = fold(total_two, got_two)
            got_two = give(total_two, sum_orders, j)
        total_one = fold(total_one, got_one)
        got_one = give(total_one, orders, j)
        if j == last_step - 1:
            total_one, gives_g = tie(total_one, gives_g)
            got_g = swap_pair(gives_g)
    total_two = fold(total_two, got_two)
    grads_two = unpack(total_two[0], middle)
    grads_two, got_one, got_g = tie(grads_two, got_one, got_g)
    total_one = fold(total_one, got_one)
    input_grad = join_pair(mine_g, got_g, 0)
    return (input_grad, *unpack(total_one[0], middle), *grads_two)


def solution(mesh):
    in_specs = (
        P(("parts", "dp"), "seq", None),
        P(("parts", "dp"), "seq", None),
        P(("seq", "dp"), None, None),
        P(("seq", "dp"), None),
        P(("seq", "dp"), None, None),
        P(("seq", "dp"), None),
    )
    out_specs = (
        P(("parts", "dp"), "seq", None),
        P(("parts", "seq", "dp"), None, None),
        P(("parts", "seq", "dp"), None),
        P(("parts", "seq", "dp"), None, None),
        P(("parts", "seq", "dp"), None),
    )
    return jax.shard_map(body, mesh=mesh, in_specs=in_specs, out_specs=out_specs, check_vma=False)
```

```python
import functools
import math

import jax
import jax.numpy as jnp
from jax import lax
from jax.experimental import pallas as pl
from jax.experimental.pallas import tpu as pltpu
from jax.sharding import PartitionSpec as P

DILATE_ONE = 64
DILATE_TWO = 128
BF = jnp.bfloat16
F32 = jnp.float32
ROOT = math.sqrt(2.0 / math.pi)
CUBE = 0.044715
VMEM = pl.BlockSpec(memory_space=pltpu.VMEM)
NT = (((1,), (1,)), ((), ()))
TN = (((0,), (0,)), ((), ()))


def gelu(v):
    return v * (0.5 * (1.0 + jnp.tanh(ROOT * (v + CUBE * (v * v * v)))))


def gelu_slope(v):
    t = jnp.tanh(ROOT * (v + CUBE * (v * v * v)))
    return 0.5 * (1.0 + t) + (0.5 * v) * (1.0 - t * t) * (ROOT * (1.0 + 3.0 * CUBE * (v * v)))


def norm_scale(v):
    return lax.rsqrt(jnp.mean(v * v, axis=-1, keepdims=True) + 1e-06)


def dot(a, b, dims=(((1,), (0,)), ((), ()))):
    return lax.dot_general(a, b, dims, preferred_element_type=F32)


def cost(flat, width, middle):
    return pl.CostEstimate(
        flops=8 * flat * width * middle, bytes_accessed=8 << 20, transcendentals=0
    )


def params():
    return pltpu.CompilerParams(vmem_limit_bytes=16 << 20)


def tie(*values):
    return lax.optimization_barrier(values)


def step_orders(count):
    bits = [1 << i for i in reversed(range(count.bit_length() - 1))]
    assert math.prod([2] * len(bits)) == count
    return bits[:-2] + bits[:-3:-1], bits


def place_of(offset, steps):
    place = 0
    for j, step in enumerate(steps):
        shift = step.bit_length() - 1
        place = place + (((offset >> shift) & 1) << j)
    return place


def cross(value):
    return lax.ppermute(value, "dp", [(0, 1), (1, 0)])


def hop(value, orders, j):
    count = lax.axis_size("seq")
    pairs = [
        (2 * i + core, 2 * (i ^ orders[core][j]) + core)
        for i in range(count)
        for core in range(2)
    ]
    return lax.ppermute(value, ("seq", "dp"), pairs)


def widen(value, got):
    return jnp.concatenate([value, got], axis=0)


def give(total, orders, j):
    return hop(total[total.shape[0] // 2 :].astype(BF), orders, j)


def fold_all(keep, got):
    return keep + got.astype(F32)


def fold(total, got):
    return total[: total.shape[0] // 2] + got.astype(F32)


def halo(first, last):
    count = lax.axis_size("seq")
    low = lax.ppermute(last, "seq", [(i, i + 2) for i in range(count - 2)])
    high = lax.ppermute(first, "seq", [(i + 2, i) for i in range(count - 2)])
    return low, high


def swap_pair(value):
    count = lax.axis_size("seq")
    return lax.ppermute(value, "seq", [(i, i ^ 1) for i in range(count)])


def ordered(leading, mine, theirs):
    return jnp.concatenate(
        [jnp.where(leading, mine, theirs), jnp.where(leading, theirs, mine)], axis=0
    )


def split_pair(field, axis):
    even = lax.axis_index("seq") % 2 == 0
    half = field.shape[axis] // 2
    low = lax.slice_in_dim(field, 0, half, axis=axis)
    high = lax.slice_in_dim(field, half, 2 * half, axis=axis)
    return jnp.where(even, low, high), jnp.where(even, high, low)


def join_pair(mine, theirs, axis):
    even = lax.axis_index("seq") % 2 == 0
    return jnp.concatenate(
        [jnp.where(even, mine, theirs), jnp.where(even, theirs, mine)], axis=axis
    )


def with_weights(pieces, orders, middle, run):
    here, core = lax.axis_index("seq"), lax.axis_index("dp")
    own, other = pieces
    count, rows = own.shape[:2]
    part = rows // 4

    def case(taps, rest):
        def whole(ref, steps, half):
            cols = slice(half * middle, (half + 1) * middle)
            return jnp.concatenate(
                [ref[place_of(here ^ chip, steps), :, cols] for chip in range(count)], axis=0
            )

        def mix(h):
            pieces = []
            for chip in range(count):
                place = place_of(here ^ chip, orders[1])
                for lane in range(2):
                    start = (2 * lane + h) * part
                    pieces.append(rest[place, start : start + part, middle:])
            return jnp.concatenate(pieces, axis=0)

        run(
            [
                lambda: whole(taps, orders[0], 0),
                lambda: whole(taps, orders[0], 1),
                lambda: whole(rest, orders[1], 0),
            ],
            [lambda: mix(0), lambda: mix(1)],
        )

    @pl.when(core == 0)
    def _():
        case(own, other)

    @pl.when(core == 1)
    def _():
        case(other, own)


def norm_rows(source, w, start, size, target, put):
    @pl.loop(0, size // 32, unroll=2)
    def _(i):
        rows = pl.multiple_of(i * 32, 32)
        v = source[w, pl.ds(start + rows, 32), :].astype(F32)
        target[w, pl.ds(put + rows, 32), :] = gelu(v * norm_scale(v)).astype(BF)


def norm_kernel(x_ref, low_ref, high_ref, ext_ref):
    dilate = low_ref.shape[1]
    length = x_ref.shape[1]
    for w in range(x_ref.shape[0]):
        norm_rows(low_ref, w, 0, dilate, ext_ref, 0)
        norm_rows(x_ref, w, 0, length, ext_ref, dilate)
        norm_rows(high_ref, w, 0, dilate, ext_ref, dilate + length)


def norm_ext(x, low, high):
    windows, length, width = x.shape
    return pl.pallas_call(
        norm_kernel,
        out_shape=jax.ShapeDtypeStruct((windows, length + 2 * low.shape[1], width), BF),
        in_specs=[VMEM] * 3,
        out_specs=VMEM,
        compiler_params=params(),
        name="norm_ext",
    )(x, low, high)


def forward_kernel(
    orders, dilate, edge, ext, x_ref, own, other, pre_ref, hid_ref, x2_ref, first_ref, last_ref
):
    pieces = (own, other)
    windows, length, width = x_ref.shape
    middle = hid_ref.shape[1]

    def run(conv, mix):
        for w in range(windows):
            rows = slice(w * length, (w + 1) * length)
            pre = sum(dot(ext[w, k * dilate : k * dilate + length, :], conv[k]()) for k in range(3))
            pre_ref[rows, :] = pre
            hid = gelu(pre).astype(BF)
            hid_ref[rows, :] = hid
            for h in range(2):
                cols = slice(h * middle, (h + 1) * middle)
                x2_ref[w, :, cols] = (x_ref[w, :, cols].astype(F32) + dot(hid, mix[h]())).astype(BF)

    with_weights(pieces, orders, middle, run)
    for w in range(windows):
        norm_rows(x2_ref, w, 0, edge, first_ref, 0)
        norm_rows(x2_ref, w, length - edge, edge, last_ref, 0)


def forward_block(ext, x, pieces, orders, dilate, edge):
    windows, length, width = x.shape
    middle = pieces[0].shape[2] // 2
    flat = windows * length
    return pl.pallas_call(
        functools.partial(forward_kernel, orders, dilate, edge),
        out_shape=(
            jax.ShapeDtypeStruct((flat, middle), F32),
            jax.ShapeDtypeStruct((flat, middle), BF),
            jax.ShapeDtypeStruct(x.shape, BF),
            jax.ShapeDtypeStruct((windows, edge, width), BF),
            jax.ShapeDtypeStruct((windows, edge, width), BF),
        ),
        in_specs=[VMEM] * 4,
        out_specs=(VMEM,) * 5,
        compiler_params=params(),
        cost_estimate=cost(flat, width, middle),
        name="forward_block",
    )(ext, x, *pieces)


def turn_kernel(
    orders, dilate, first, last, low, high, x_ref, e_ref, own, other,
    ext, hid_ref, dpre_ref, dfirst, dlast,
):
    pieces = (own, other)
    windows, length, width = e_ref.shape
    edge = first.shape[1]
    middle = hid_ref.shape[1]
    for w in range(windows):
        for source, start in (
            (low, 0), (first, dilate), (last, dilate + length - edge), (high, dilate + length),
        ):
            ext[w, start : start + edge, :] = source[w]
        norm_rows(x_ref, w, edge, length - 2 * edge, ext, dilate + edge)

    def run(conv, mix):
        for w in range(windows):
            rows = slice(w * length, (w + 1) * length)
            pre = sum(dot(ext[w, k * dilate : k * dilate + length, :], conv[k]()) for k in range(3))
            dhid = dot(e_ref[w, :, :middle], mix[0](), NT) + dot(e_ref[w, :, middle:], mix[1](), NT)
            hid_ref[rows, :] = gelu(pre).astype(BF)
            dpre_ref[rows, :] = (gelu_slope(pre) * dhid).astype(BF)

    with_weights(pieces, orders, middle, run)
    for w in range(windows):
        dfirst[w] = dpre_ref[w * length : w * length + dilate, :]
        dlast[w] = dpre_ref[(w + 1) * length - dilate : (w + 1) * length, :]


def turn_block(first, last, low, high, x, e, pieces, orders, dilate):
    windows, length, width = e.shape
    middle = pieces[0].shape[2] // 2
    flat = windows * length
    return pl.pallas_call(
        functools.partial(turn_kernel, orders, dilate),
        out_shape=(
            jax.ShapeDtypeStruct((windows, length + 2 * dilate, width), BF),
            jax.ShapeDtypeStruct((flat, middle), BF),
            jax.ShapeDtypeStruct((flat, middle), BF),
            jax.ShapeDtypeStruct((windows, dilate, middle), BF),
            jax.ShapeDtypeStruct((windows, dilate, middle), BF),
        ),
        in_specs=[VMEM] * 8,
        out_specs=(VMEM,) * 5,
        compiler_params=params(),
        cost_estimate=cost(flat, width, middle),
        name="turn_block",
    )(first, last, low, high, x, e, *pieces)


def grads_kernel(orders, dilate, ext, hid, e_ref, dpre, keep, send, full):
    here, core = lax.axis_index("seq"), lax.axis_index("dp")
    windows, length, width = e_ref.shape
    middle = hid.shape[1]
    count, rows = keep.shape[:2]
    part = rows // 4

    def put(target, k):
        steps = orders[k // 2]
        cols = slice((k % 2) * middle, (k % 2 + 1) * middle)
        for chip in range(count):
            place = place_of(here ^ chip, steps)
            if k < 3:
                value = full[chip * rows : (chip + 1) * rows, :]
                target[place, :, cols] = value.astype(target.dtype)
                continue
            for lane in range(2):
                for h in range(2):
                    base = h * middle + (2 * chip + lane) * part
                    start = (2 * lane + h) * part
                    value = full[base : base + part, :]
                    target[place, start : start + part, cols] = value.astype(target.dtype)

    for k in range(4):
        if k == 3:
            for h in range(2):
                e = jnp.concatenate(
                    [e_ref[w, :, h * middle : (h + 1) * middle] for w in range(windows)], axis=0
                )
                full[h * middle : (h + 1) * middle, :] = dot(hid[...], e, TN)
        else:
            view = jnp.concatenate(
                [ext[w, k * dilate : k * dilate + length, :] for w in range(windows)], axis=0
            )
            full[...] = dot(view, dpre[...], TN)

        @pl.when(core == k // 2)
        def _():
            put(keep, k)

        @pl.when(core != k // 2)
        def _():
            put(send, k)


def grads_block(ext, hid, e, dpre, orders, dilate, count):
    windows, length, width = e.shape
    flat, middle = hid.shape
    shape = (count, width // count, 2 * middle)
    return pl.pallas_call(
        functools.partial(grads_kernel, orders, dilate),
        out_shape=(jax.ShapeDtypeStruct(shape, F32), jax.ShapeDtypeStruct(shape, BF)),
        in_specs=[VMEM] * 4,
        out_specs=(VMEM,) * 2,
        scratch_shapes=[pltpu.VMEM((width, middle), F32)],
        compiler_params=params(),
        cost_estimate=cost(flat, width, middle),
        name="grads_block",
    )(ext, hid, e, dpre)


def back_kernel(orders, dilate, chained, *refs):
    dpre, low, high, x_ref, e_ref = refs[:5]
    pieces = refs[5:7]
    if chained:
        pieces_m = refs[7:9]
        pre_ref, out_ref, dprev, dfirst, dlast, ext, dn = refs[9:]
    else:
        out_ref, ext, dn = refs[7:]
    windows, length, width = x_ref.shape
    middle = dpre.shape[1]
    for w in range(windows):
        ext[w, :dilate, :] = low[w]
        ext[w, dilate : dilate + length, :] = dpre[w * length : (w + 1) * length, :]
        ext[w, dilate + length :, :] = high[w]

    def run(conv, mix):
        for w in range(windows):
            dn[w] = sum(
                dot(ext[w, (2 - k) * dilate : (2 - k) * dilate + length, :], conv[k](), NT)
                for k in range(3)
            )

    with_weights(pieces, orders, middle, run)
    for w in range(windows):

        @pl.loop(0, length // 32, unroll=2)
        def _(i):
            rows = pl.ds(pl.multiple_of(i * 32, 32), 32)
            v = x_ref[w, rows, :].astype(F32)
            scale = norm_scale(v)
            u = v * scale
            g = dn[w, rows, :] * gelu_slope(u)
            dv = scale * (g - u * jnp.mean(g * u, axis=-1, keepdims=True))
            out_ref[w, rows, :] = (e_ref[w, rows, :].astype(F32) + dv).astype(BF)

    if chained:

        def turn(conv, mix):
            for w in range(windows):
                dhid = dot(out_ref[w, :, :middle], mix[0](), NT) + dot(
                    out_ref[w, :, middle:], mix[1](), NT
                )
                rows = slice(w * length, (w + 1) * length)
                dprev[rows, :] = (gelu_slope(pre_ref[rows, :]) * dhid).astype(BF)

        with_weights(pieces_m, orders, middle, turn)
        edge = dfirst.shape[1]
        for w in range(windows):
            dfirst[w] = dprev[w * length : w * length + edge, :]
            dlast[w] = dprev[(w + 1) * length - edge : (w + 1) * length, :]


def back_block(dpre, low, high, x, e, pieces, orders, dilate, previous=None):
    windows, length, width = x.shape
    flat, middle = dpre.shape
    chained = previous is not None
    operands = [dpre, low, high, x, e, *pieces]
    shapes = [jax.ShapeDtypeStruct(x.shape, BF)]
    if chained:
        others, pre, edge = previous
        operands += [*others, pre]
        shapes += [
            jax.ShapeDtypeStruct((flat, middle), BF),
            jax.ShapeDtypeStruct((windows, edge, middle), BF),
            jax.ShapeDtypeStruct((windows, edge, middle), BF),
        ]
    return pl.pallas_call(
        functools.partial(back_kernel, orders, dilate, chained),
        out_shape=tuple(shapes),
        in_specs=[VMEM] * len(operands),
        out_specs=(VMEM,) * len(shapes),
        scratch_shapes=[
            pltpu.VMEM((windows, length + 2 * dilate, middle), BF),
            pltpu.VMEM((windows, length, width), F32),
        ],
        compiler_params=params(),
        cost_estimate=cost(flat, width, middle),
        name="back_block",
    )(*operands)


def pack(conv, mix):
    middle = conv.shape[2]
    first = conv[:, :2].reshape(conv.shape[0], 2 * middle)
    tall = jnp.concatenate([mix[:, :middle], mix[:, middle:]], axis=0)
    second = jnp.concatenate([conv[:, 2], tall], axis=1)
    return first, second


def unpack(total, middle):
    rows = total.shape[0] // 2
    leading = lax.axis_index("dp") == 0
    got = cross(jnp.where(leading, total[rows:], total[:rows]))
    first = jnp.where(leading, total[:rows], got)
    second = jnp.where(leading, got, total[rows:])
    conv = jnp.concatenate(
        [first.reshape(rows, 2, middle), second[:, None, :middle]], axis=1
    )
    half = rows // 2
    mix = jnp.concatenate([second[:half, middle:], second[half:, middle:]], axis=1)
    return conv, mix


def body(activations, cotangent, conv_one, mix_one, conv_two, mix_two):
    count = lax.axis_size("seq")
    orders = step_orders(count)
    sum_orders = orders
    last_step = len(orders[0]) - 1
    middle = conv_one.shape[2]
    leading = lax.axis_index("dp") == 0

    def chip_part(conv, mix):
        first, second = pack(conv, mix)
        got = cross(jnp.where(leading, second, first))
        return ordered(leading, jnp.where(leading, first, second), got)[None]

    mine_x, gives_x = split_pair(activations, 0)
    got_x = swap_pair(gives_x)
    own_one = chip_part(conv_one, mix_one)
    got_one = hop(own_one, orders, 0)
    conv_two, mix_two, own_one = tie(conv_two, mix_two, own_one)
    own_two = chip_part(conv_two, mix_two)
    own_one = widen(own_one, got_one)
    got_one = hop(own_one, orders, 1)
    got_two = hop(own_two, orders, 0)
    own_one, cotangent, got_x = tie(own_one, cotangent, got_x)
    x = join_pair(mine_x, got_x, 1)
    length = x.shape[1]
    low, high = halo(x[:, :DILATE_ONE], x[:, length - DILATE_ONE :])
    mine_e, gives_e = split_pair(cotangent, 0)
    got_e = swap_pair(gives_e)
    ext_one = norm_ext(x, low, high)
    got_one, got_two, ext_one, got_e = tie(got_one, got_two, ext_one, got_e)
    for j in range(2, last_step + 1):
        own_one, own_two = widen(own_one, got_one), widen(own_two, got_two)
        got_one, got_two = hop(own_one, orders, j), hop(own_two, orders, j - 1)
        if j == last_step:
            e = join_pair(mine_e, got_e, 1)
        got_one, got_two = tie(got_one, got_two)
    own_one = widen(own_one, got_one)
    got_one = cross(own_one)
    own_one, got_two = tie(own_one, got_two)
    own_two = widen(own_two, got_two)
    got_two = hop(own_two, orders, last_step)
    pieces_one = (own_one, got_one)
    pre_one, hid_one, second_in, first, last = forward_block(
        ext_one, x, pieces_one, orders, DILATE_ONE, DILATE_TWO
    )
    low, high = halo(first, last)
    got_two, low, high = tie(got_two, low, high)
    own_two = widen(own_two, got_two)
    pieces_two = (own_two, cross(own_two))
    ext_two, hid_two, dpre_two, dfirst, dlast = turn_block(
        first, last, low, high, second_in, e, pieces_two, orders, DILATE_TWO
    )

    dlow, dhigh = halo(dfirst, dlast)
    keep_two, send = grads_block(
        ext_two, hid_two, e, dpre_two, sum_orders, DILATE_TWO, count
    )
    dlow, dhigh, send = tie(dlow, dhigh, send)
    got_two = cross(send)
    total_two = fold_all(keep_two, got_two)
    total_two, dlow, dhigh = tie(total_two, dlow, dhigh)
    got_two = give(total_two, sum_orders, last_step)
    upstream, dpre_one, dfirst, dlast = back_block(
        dpre_two, dlow, dhigh, second_in, e, pieces_two, orders, DILATE_TWO,
        (pieces_one, pre_one, DILATE_ONE),
    )
    keep_one, send = grads_block(ext_one, hid_one, upstream, dpre_one, orders, DILATE_ONE, count)
    got_two, send, dfirst, dlast = tie(got_two, send, dfirst, dlast)
    got_one = cross(send)
    dlow, dhigh = halo(dfirst, dlast)
    total_two = fold(total_two, got_two)
    got_two = give(total_two, sum_orders, last_step - 1)
    total_one = fold_all(keep_one, got_one)
    total_one, total_two, dlow, dhigh = tie(total_one, total_two, dlow, dhigh)
    got_one = give(total_one, orders, last_step)
    (input_grad,) = back_block(
        dpre_one, dlow, dhigh, x, upstream, pieces_one, orders, DILATE_ONE
    )
    input_grad, got_one, got_two = tie(input_grad, got_one, got_two)
    mine_g, gives_g = split_pair(input_grad, 1)
    for j in reversed(range(last_step)):
        if j < last_step - 1:
            total_two = fold(total_two, got_two)
            got_two = give(total_two, sum_orders, j)
        total_one = fold(total_one, got_one)
        got_one = give(total_one, orders, j)
        if j == last_step - 1:
            got_one, gives_g = tie(got_one, gives_g)
            got_g = swap_pair(gives_g)
    total_two = fold(total_two, got_two)
    grads_two = unpack(total_two[0], middle)
    grads_two, got_one, got_g = tie(grads_two, got_one, got_g)
    total_one = fold(total_one, got_one)
    input_grad = join_pair(mine_g, got_g, 0)
    return (input_grad, *unpack(total_one[0], middle), *grads_two)


def solution(mesh):
    in_specs = (
        P(("parts", "dp"), "seq", None),
        P(("parts", "dp"), "seq", None),
        P(("seq", "dp"), None, None),
        P(("seq", "dp"), None),
        P(("seq", "dp"), None, None),
        P(("seq", "dp"), None),
    )
    out_specs = (
        P(("parts", "dp"), "seq", None),
        P(("parts", "seq", "dp"), None, None),
        P(("parts", "seq", "dp"), None),
        P(("parts", "seq", "dp"), None, None),
        P(("parts", "seq", "dp"), None),
    )
    return jax.shard_map(body, mesh=mesh, in_specs=in_specs, out_specs=out_specs, check_vma=False)
```

```python
import functools
import math

import jax
import jax.numpy as jnp
from jax import lax
from jax.experimental import pallas as pl
from jax.experimental.pallas import tpu as pltpu
from jax.sharding import PartitionSpec as P

DILATE_ONE = 64
DILATE_TWO = 128
BF = jnp.bfloat16
F32 = jnp.float32
GATHER_ONE = ((0, 2, 1), (0, 1, 2))
GATHER_TWO = ((0, 2, 1), (0, 1, 2))
SUM_ONE = ((0, 2, 1), (0, 1, 2))
SUM_TWO = ((0, 2, 1), (1, 0, 2))
ROOT = math.sqrt(2.0 / math.pi)
CUBE = 0.044715
VMEM = pl.BlockSpec(memory_space=pltpu.VMEM)
NT = (((1,), (1,)), ((), ()))
TN = (((0,), (0,)), ((), ()))


def gelu(v):
    return v * (0.5 * (1.0 + jnp.tanh(ROOT * (v + CUBE * (v * v * v)))))


def gelu_slope(v):
    t = jnp.tanh(ROOT * (v + CUBE * (v * v * v)))
    return 0.5 * (1.0 + t) + (0.5 * v) * (1.0 - t * t) * (ROOT * (1.0 + 3.0 * CUBE * (v * v)))


def norm_scale(v):
    return lax.rsqrt(jnp.mean(v * v, axis=-1, keepdims=True) + 1e-06)


def dot(a, b, dims=(((1,), (0,)), ((), ()))):
    return lax.dot_general(a, b, dims, preferred_element_type=F32)


def cost(flat, width, middle):
    return pl.CostEstimate(
        flops=8 * flat * width * middle, bytes_accessed=8 << 20, transcendentals=0
    )


def params():
    return pltpu.CompilerParams(vmem_limit_bytes=16 << 20)


def tie(*values):
    return lax.optimization_barrier(values)


def step_orders(count, ranks):
    bits = [1 << i for i in reversed(range(count.bit_length() - 1))]
    assert math.prod([2] * len(bits)) == count
    if len(bits) == len(ranks[0]):
        return tuple([bits[i] for i in order] for order in ranks)
    return bits[:-2] + bits[:-3:-1], bits


def place_of(offset, steps):
    place = 0
    for j, step in enumerate(steps):
        shift = step.bit_length() - 1
        place = place + (((offset >> shift) & 1) << j)
    return place


def cross(value):
    return lax.ppermute(value, "dp", [(0, 1), (1, 0)])


def hop(value, orders, j):
    count = lax.axis_size("seq")
    pairs = [
        (2 * i + core, 2 * (i ^ orders[core][j]) + core)
        for i in range(count)
        for core in range(2)
    ]
    return lax.ppermute(value, ("seq", "dp"), pairs)


def widen(value, got):
    return jnp.concatenate([value, got], axis=0)


def give(total, orders, j):
    return hop(total[total.shape[0] // 2 :].astype(BF), orders, j)


def fold_all(keep, got):
    return keep + got.astype(F32)


def fold(total, got):
    return total[: total.shape[0] // 2] + got.astype(F32)


def halo(first, last):
    count = lax.axis_size("seq")
    low = lax.ppermute(last, "seq", [(i, i + 2) for i in range(count - 2)])
    high = lax.ppermute(first, "seq", [(i + 2, i) for i in range(count - 2)])
    return low, high


def swap_pair(value):
    count = lax.axis_size("seq")
    return lax.ppermute(value, "seq", [(i, i ^ 1) for i in range(count)])


def ordered(leading, mine, theirs):
    return jnp.concatenate(
        [jnp.where(leading, mine, theirs), jnp.where(leading, theirs, mine)], axis=0
    )


def split_pair(field, axis):
    even = lax.axis_index("seq") % 2 == 0
    half = field.shape[axis] // 2
    low = lax.slice_in_dim(field, 0, half, axis=axis)
    high = lax.slice_in_dim(field, half, 2 * half, axis=axis)
    return jnp.where(even, low, high), jnp.where(even, high, low)


def join_pair(mine, theirs, axis):
    even = lax.axis_index("seq") % 2 == 0
    return jnp.concatenate(
        [jnp.where(even, mine, theirs), jnp.where(even, theirs, mine)], axis=axis
    )


def with_weights(pieces, orders, middle, run):
    here, core = lax.axis_index("seq"), lax.axis_index("dp")
    own, other = pieces
    count, rows = own.shape[:2]
    part = rows // 4

    def case(taps, rest):
        def whole(ref, steps, half):
            cols = slice(half * middle, (half + 1) * middle)
            return jnp.concatenate(
                [ref[place_of(here ^ chip, steps), :, cols] for chip in range(count)], axis=0
            )

        def mix(h):
            pieces = []
            for chip in range(count):
                place = place_of(here ^ chip, orders[1])
                for lane in range(2):
                    start = (2 * lane + h) * part
                    pieces.append(rest[place, start : start + part, middle:])
            return jnp.concatenate(pieces, axis=0)

        run(
            [
                lambda: whole(taps, orders[0], 0),
                lambda: whole(taps, orders[0], 1),
                lambda: whole(rest, orders[1], 0),
            ],
            [lambda: mix(0), lambda: mix(1)],
        )

    @pl.when(core == 0)
    def _():
        case(own, other)

    @pl.when(core == 1)
    def _():
        case(other, own)


def norm_rows(source, w, start, size, target, put):
    @pl.loop(0, size // 32, unroll=4)
    def _(i):
        rows = pl.multiple_of(i * 32, 32)
        v = source[w, pl.ds(start + rows, 32), :].astype(F32)
        target[w, pl.ds(put + rows, 32), :] = gelu(v * norm_scale(v)).astype(BF)


def norm_kernel(x_ref, low_ref, high_ref, ext_ref):
    dilate = low_ref.shape[1]
    length = x_ref.shape[1]
    for w in range(x_ref.shape[0]):
        norm_rows(low_ref, w, 0, dilate, ext_ref, 0)
        norm_rows(x_ref, w, 0, length, ext_ref, dilate)
        norm_rows(high_ref, w, 0, dilate, ext_ref, dilate + length)


def norm_ext(x, low, high):
    windows, length, width = x.shape
    return pl.pallas_call(
        norm_kernel,
        out_shape=jax.ShapeDtypeStruct((windows, length + 2 * low.shape[1], width), BF),
        in_specs=[VMEM] * 3,
        out_specs=VMEM,
        compiler_params=params(),
        name="norm_ext",
    )(x, low, high)


def forward_kernel(
    orders, dilate, edge, ext, x_ref, own, other, pre_ref, hid_ref, x2_ref, first_ref, last_ref
):
    pieces = (own, other)
    windows, length, width = x_ref.shape
    middle = hid_ref.shape[1]

    def run(conv, mix):
        for w in range(windows):
            rows = slice(w * length, (w + 1) * length)
            pre = sum(dot(ext[w, k * dilate : k * dilate + length, :], conv[k]()) for k in range(3))
            pre_ref[rows, :] = pre
            hid = gelu(pre).astype(BF)
            hid_ref[rows, :] = hid
            for h in range(2):
                cols = slice(h * middle, (h + 1) * middle)
                x2_ref[w, :, cols] = (x_ref[w, :, cols].astype(F32) + dot(hid, mix[h]())).astype(BF)

    with_weights(pieces, orders, middle, run)
    for w in range(windows):
        norm_rows(x2_ref, w, 0, edge, first_ref, 0)
        norm_rows(x2_ref, w, length - edge, edge, last_ref, 0)


def forward_block(ext, x, pieces, orders, dilate, edge):
    windows, length, width = x.shape
    middle = pieces[0].shape[2] // 2
    flat = windows * length
    return pl.pallas_call(
        functools.partial(forward_kernel, orders, dilate, edge),
        out_shape=(
            jax.ShapeDtypeStruct((flat, middle), F32),
            jax.ShapeDtypeStruct((flat, middle), BF),
            jax.ShapeDtypeStruct(x.shape, BF),
            jax.ShapeDtypeStruct((windows, edge, width), BF),
            jax.ShapeDtypeStruct((windows, edge, width), BF),
        ),
        in_specs=[VMEM] * 4,
        out_specs=(VMEM,) * 5,
        compiler_params=params(),
        cost_estimate=cost(flat, width, middle),
        name="forward_block",
    )(ext, x, *pieces)


def turn_kernel(
    orders, dilate, first, last, low, high, x_ref, e_ref, own, other,
    ext, hid_ref, dpre_ref, dfirst, dlast,
):
    pieces = (own, other)
    windows, length, width = e_ref.shape
    edge = first.shape[1]
    middle = hid_ref.shape[1]
    for w in range(windows):
        for source, start in (
            (low, 0), (first, dilate), (last, dilate + length - edge), (high, dilate + length),
        ):
            ext[w, start : start + edge, :] = source[w]
        norm_rows(x_ref, w, edge, length - 2 * edge, ext, dilate + edge)

    def run(conv, mix):
        for w in range(windows):
            rows = slice(w * length, (w + 1) * length)
            pre = sum(dot(ext[w, k * dilate : k * dilate + length, :], conv[k]()) for k in range(3))
            dhid = dot(e_ref[w, :, :middle], mix[0](), NT) + dot(e_ref[w, :, middle:], mix[1](), NT)
            hid_ref[rows, :] = gelu(pre).astype(BF)
            dpre_ref[rows, :] = (gelu_slope(pre) * dhid).astype(BF)

    with_weights(pieces, orders, middle, run)
    for w in range(windows):
        dfirst[w] = dpre_ref[w * length : w * length + dilate, :]
        dlast[w] = dpre_ref[(w + 1) * length - dilate : (w + 1) * length, :]


def turn_block(first, last, low, high, x, e, pieces, orders, dilate):
    windows, length, width = e.shape
    middle = pieces[0].shape[2] // 2
    flat = windows * length
    return pl.pallas_call(
        functools.partial(turn_kernel, orders, dilate),
        out_shape=(
            jax.ShapeDtypeStruct((windows, length + 2 * dilate, width), BF),
            jax.ShapeDtypeStruct((flat, middle), BF),
            jax.ShapeDtypeStruct((flat, middle), BF),
            jax.ShapeDtypeStruct((windows, dilate, middle), BF),
            jax.ShapeDtypeStruct((windows, dilate, middle), BF),
        ),
        in_specs=[VMEM] * 8,
        out_specs=(VMEM,) * 5,
        compiler_params=params(),
        cost_estimate=cost(flat, width, middle),
        name="turn_block",
    )(first, last, low, high, x, e, *pieces)


def grads_kernel(orders, dilate, ext, hid, e_ref, dpre, keep, send, full):
    here, core = lax.axis_index("seq"), lax.axis_index("dp")
    windows, length, width = e_ref.shape
    middle = hid.shape[1]
    count, rows = keep.shape[:2]
    part = rows // 4

    def put(target, k):
        steps = orders[k // 2]
        cols = slice((k % 2) * middle, (k % 2 + 1) * middle)
        for chip in range(count):
            place = place_of(here ^ chip, steps)
            if k < 3:
                value = full[chip * rows : (chip + 1) * rows, :]
                target[place, :, cols] = value.astype(target.dtype)
                continue
            for lane in range(2):
                for h in range(2):
                    base = h * middle + (2 * chip + lane) * part
                    start = (2 * lane + h) * part
                    value = full[base : base + part, :]
                    target[place, start : start + part, cols] = value.astype(target.dtype)

    for k in range(4):
        if k == 3:
            for h in range(2):
                e = jnp.concatenate(
                    [e_ref[w, :, h * middle : (h + 1) * middle] for w in range(windows)], axis=0
                )
                full[h * middle : (h + 1) * middle, :] = dot(hid[...], e, TN)
        else:
            view = jnp.concatenate(
                [ext[w, k * dilate : k * dilate + length, :] for w in range(windows)], axis=0
            )
            full[...] = dot(view, dpre[...], TN)

        @pl.when(core == k // 2)
        def _():
            put(keep, k)

        @pl.when(core != k // 2)
        def _():
            put(send, k)


def grads_block(ext, hid, e, dpre, orders, dilate, count):
    windows, length, width = e.shape
    flat, middle = hid.shape
    shape = (count, width // count, 2 * middle)
    return pl.pallas_call(
        functools.partial(grads_kernel, orders, dilate),
        out_shape=(jax.ShapeDtypeStruct(shape, F32), jax.ShapeDtypeStruct(shape, BF)),
        in_specs=[VMEM] * 4,
        out_specs=(VMEM,) * 2,
        scratch_shapes=[pltpu.VMEM((width, middle), F32)],
        compiler_params=params(),
        cost_estimate=cost(flat, width, middle),
        name="grads_block",
    )(ext, hid, e, dpre)


def back_kernel(orders, dilate, orders_m, *refs):
    chained = orders_m is not None
    dpre, low, high, x_ref, e_ref = refs[:5]
    pieces = refs[5:7]
    if chained:
        pieces_m = refs[7:9]
        pre_ref, out_ref, dprev, dfirst, dlast, ext, dn = refs[9:]
    else:
        out_ref, ext, dn = refs[7:]
    windows, length, width = x_ref.shape
    middle = dpre.shape[1]
    for w in range(windows):
        ext[w, :dilate, :] = low[w]
        ext[w, dilate : dilate + length, :] = dpre[w * length : (w + 1) * length, :]
        ext[w, dilate + length :, :] = high[w]

    def run(conv, mix):
        for w in range(windows):
            dn[w] = sum(
                dot(ext[w, (2 - k) * dilate : (2 - k) * dilate + length, :], conv[k](), NT)
                for k in range(3)
            )

    with_weights(pieces, orders, middle, run)
    for w in range(windows):

        @pl.loop(0, length // 32, unroll=4)
        def _(i):
            rows = pl.ds(pl.multiple_of(i * 32, 32), 32)
            v = x_ref[w, rows, :].astype(F32)
            scale = norm_scale(v)
            u = v * scale
            g = dn[w, rows, :] * gelu_slope(u)
            dv = scale * (g - u * jnp.mean(g * u, axis=-1, keepdims=True))
            out_ref[w, rows, :] = (e_ref[w, rows, :].astype(F32) + dv).astype(BF)

    if chained:

        def turn(conv, mix):
            for w in range(windows):
                dhid = dot(out_ref[w, :, :middle], mix[0](), NT) + dot(
                    out_ref[w, :, middle:], mix[1](), NT
                )
                rows = slice(w * length, (w + 1) * length)
                dprev[rows, :] = (gelu_slope(pre_ref[rows, :]) * dhid).astype(BF)

        with_weights(pieces_m, orders_m, middle, turn)
        edge = dfirst.shape[1]
        for w in range(windows):
            dfirst[w] = dprev[w * length : w * length + edge, :]
            dlast[w] = dprev[(w + 1) * length - edge : (w + 1) * length, :]


def back_block(dpre, low, high, x, e, pieces, orders, dilate, previous=None):
    windows, length, width = x.shape
    flat, middle = dpre.shape
    chained, orders_m = previous is not None, None
    operands = [dpre, low, high, x, e, *pieces]
    shapes = [jax.ShapeDtypeStruct(x.shape, BF)]
    if chained:
        others, orders_m, pre, edge = previous
        operands += [*others, pre]
        shapes += [
            jax.ShapeDtypeStruct((flat, middle), BF),
            jax.ShapeDtypeStruct((windows, edge, middle), BF),
            jax.ShapeDtypeStruct((windows, edge, middle), BF),
        ]
    return pl.pallas_call(
        functools.partial(back_kernel, orders, dilate, orders_m),
        out_shape=tuple(shapes),
        in_specs=[VMEM] * len(operands),
        out_specs=(VMEM,) * len(shapes),
        scratch_shapes=[
            pltpu.VMEM((windows, length + 2 * dilate, middle), BF),
            pltpu.VMEM((windows, length, width), F32),
        ],
        compiler_params=params(),
        cost_estimate=cost(flat, width, middle),
        name="back_block",
    )(*operands)


def pack(conv, mix):
    middle = conv.shape[2]
    first = conv[:, :2].reshape(conv.shape[0], 2 * middle)
    tall = jnp.concatenate([mix[:, :middle], mix[:, middle:]], axis=0)
    second = jnp.concatenate([conv[:, 2], tall], axis=1)
    return first, second


def unpack(total, middle):
    rows = total.shape[0] // 2
    leading = lax.axis_index("dp") == 0
    got = cross(jnp.where(leading, total[rows:], total[:rows]))
    first = jnp.where(leading, total[:rows], got)
    second = jnp.where(leading, got, total[rows:])
    conv = jnp.concatenate(
        [first.reshape(rows, 2, middle), second[:, None, :middle]], axis=1
    )
    half = rows // 2
    mix = jnp.concatenate([second[:half, middle:], second[half:, middle:]], axis=1)
    return conv, mix


def body(activations, cotangent, conv_one, mix_one, conv_two, mix_two):
    count = lax.axis_size("seq")
    orders = step_orders(count, GATHER_ONE)
    orders_two = step_orders(count, GATHER_TWO)
    sums_one = step_orders(count, SUM_ONE)
    sums_two = step_orders(count, SUM_TWO)
    last_step = len(orders[0]) - 1
    middle = conv_one.shape[2]
    leading = lax.axis_index("dp") == 0

    def chip_part(conv, mix):
        first, second = pack(conv, mix)
        got = cross(jnp.where(leading, second, first))
        return ordered(leading, jnp.where(leading, first, second), got)[None]

    mine_x, gives_x = split_pair(activations, 0)
    got_x = swap_pair(gives_x)
    own_one = chip_part(conv_one, mix_one)
    got_one = hop(own_one, orders, 0)
    conv_two, mix_two, own_one = tie(conv_two, mix_two, own_one)
    own_two = chip_part(conv_two, mix_two)
    own_one = widen(own_one, got_one)
    got_one = hop(own_one, orders, 1)
    got_two = hop(own_two, orders_two, 0)
    own_one, cotangent, got_x = tie(own_one, cotangent, got_x)
    x = join_pair(mine_x, got_x, 1)
    length = x.shape[1]
    low, high = halo(x[:, :DILATE_ONE], x[:, length - DILATE_ONE :])
    mine_e, gives_e = split_pair(cotangent, 0)
    got_e = swap_pair(gives_e)
    ext_one = norm_ext(x, low, high)
    got_one, got_two, ext_one, got_e = tie(got_one, got_two, ext_one, got_e)
    for j in range(2, last_step + 1):
        own_one, own_two = widen(own_one, got_one), widen(own_two, got_two)
        got_one, got_two = hop(own_one, orders, j), hop(own_two, orders_two, j - 1)
        if j == last_step:
            e = join_pair(mine_e, got_e, 1)
        got_one, got_two = tie(got_one, got_two)
    own_one = widen(own_one, got_one)
    got_one = cross(own_one)
    own_one, got_two = tie(own_one, got_two)
    own_two = widen(own_two, got_two)
    got_two = hop(own_two, orders_two, last_step)
    pieces_one = (own_one, got_one)
    pre_one, hid_one, second_in, first, last = forward_block(
        ext_one, x, pieces_one, orders, DILATE_ONE, DILATE_TWO
    )
    low, high = halo(first, last)
    got_two, low, high = tie(got_two, low, high)
    own_two = widen(own_two, got_two)
    pieces_two = (own_two, cross(own_two))
    ext_two, hid_two, dpre_two, dfirst, dlast = turn_block(
        first, last, low, high, second_in, e, pieces_two, orders_two, DILATE_TWO
    )

    dlow, dhigh = halo(dfirst, dlast)
    keep_two, send = grads_block(
        ext_two, hid_two, e, dpre_two, sums_two, DILATE_TWO, count
    )
    dlow, dhigh, send = tie(dlow, dhigh, send)
    got_two = cross(send)
    upstream, dpre_one, dfirst, dlast = back_block(
        dpre_two, dlow, dhigh, second_in, e, pieces_two, orders_two, DILATE_TWO,
        (pieces_one, orders, pre_one, DILATE_ONE),
    )
    got_two, dpre_one, upstream = tie(got_two, dpre_one, upstream)
    total_two = fold_all(keep_two, got_two)
    total_two, dpre_one = tie(total_two, dpre_one)
    got_two = give(total_two, sums_two, last_step)
    keep_one, send = grads_block(ext_one, hid_one, upstream, dpre_one, sums_one, DILATE_ONE, count)
    got_one = cross(send)
    dfirst, dlast, send = tie(dfirst, dlast, send)
    dlow, dhigh = halo(dfirst, dlast)
    total_one = fold_all(keep_one, got_one)
    got_two, total_one, dlow, dhigh = tie(got_two, total_one, dlow, dhigh)
    got_one = give(total_one, sums_one, last_step)
    total_two = fold(total_two, got_two)
    got_two = give(total_two, sums_two, last_step - 1)
    (input_grad,) = back_block(
        dpre_one, dlow, dhigh, x, upstream, pieces_one, orders, DILATE_ONE
    )
    input_grad, got_one, got_two = tie(input_grad, got_one, got_two)
    mine_g, gives_g = split_pair(input_grad, 1)
    for j in reversed(range(last_step)):
        if j < last_step - 1:
            total_two = fold(total_two, got_two)
            got_two = give(total_two, sums_two, j)
        total_one = fold(total_one, got_one)
        got_one = give(total_one, sums_one, j)
        if j == last_step - 1:
            got_one, gives_g = tie(got_one, gives_g)
            got_g = swap_pair(gives_g)
    total_two = fold(total_two, got_two)
    grads_two = unpack(total_two[0], middle)
    grads_two, got_one, got_g = tie(grads_two, got_one, got_g)
    total_one = fold(total_one, got_one)
    input_grad = join_pair(mine_g, got_g, 0)
    return (input_grad, *unpack(total_one[0], middle), *grads_two)


def solution(mesh):
    in_specs = (
        P(("parts", "dp"), "seq", None),
        P(("parts", "dp"), "seq", None),
        P(("seq", "dp"), None, None),
        P(("seq", "dp"), None),
        P(("seq", "dp"), None, None),
        P(("seq", "dp"), None),
    )
    out_specs = (
        P(("parts", "dp"), "seq", None),
        P(("parts", "seq", "dp"), None, None),
        P(("parts", "seq", "dp"), None),
        P(("parts", "seq", "dp"), None, None),
        P(("parts", "seq", "dp"), None),
    )
    return jax.shard_map(body, mesh=mesh, in_specs=in_specs, out_specs=out_specs, check_vma=False)
```

```python
import functools
import math

import jax
import jax.numpy as jnp
from jax import lax
from jax.experimental import pallas as pl
from jax.experimental.pallas import tpu as pltpu
from jax.sharding import PartitionSpec as P

DILATE_ONE = 64
DILATE_TWO = 128
BF = jnp.bfloat16
F32 = jnp.float32
GATHER_ONE = ((0, 2, 1), (0, 1, 2))
GATHER_TWO = ((0, 2, 1), (0, 1, 2))
SUM_ONE = ((0, 2, 1), (0, 1, 2))
SUM_TWO = ((0, 2, 1), (1, 0, 2))
ROOT = math.sqrt(2.0 / math.pi)
CUBE = 0.044715
VMEM = pl.BlockSpec(memory_space=pltpu.VMEM)
NT = (((1,), (1,)), ((), ()))
TN = (((0,), (0,)), ((), ()))


def gelu(v):
    return v * (0.5 * (1.0 + jnp.tanh(ROOT * (v + CUBE * (v * v * v)))))


def gelu_slope(v):
    t = jnp.tanh(ROOT * (v + CUBE * (v * v * v)))
    return 0.5 * (1.0 + t) + (0.5 * v) * (1.0 - t * t) * (ROOT * (1.0 + 3.0 * CUBE * (v * v)))


def norm_scale(v):
    return lax.rsqrt(jnp.mean(v * v, axis=-1, keepdims=True) + 1e-06)


def dot(a, b, dims=(((1,), (0,)), ((), ()))):
    return lax.dot_general(a, b, dims, preferred_element_type=F32)


def cost(flat, width, middle):
    return pl.CostEstimate(
        flops=8 * flat * width * middle, bytes_accessed=8 << 20, transcendentals=0
    )


def params():
    return pltpu.CompilerParams(vmem_limit_bytes=16 << 20)


def tie(*values):
    return lax.optimization_barrier(values)


def step_orders(count, ranks):
    bits = [1 << i for i in reversed(range(count.bit_length() - 1))]
    assert math.prod([2] * len(bits)) == count
    if len(bits) == len(ranks[0]):
        return tuple([bits[i] for i in order] for order in ranks)
    return bits[:-2] + bits[:-3:-1], bits


def place_of(offset, steps):
    place = 0
    for j, step in enumerate(steps):
        shift = step.bit_length() - 1
        place = place + (((offset >> shift) & 1) << j)
    return place


def cross(value):
    return lax.ppermute(value, "dp", [(0, 1), (1, 0)])


def hop(value, orders, j):
    count = lax.axis_size("seq")
    pairs = [
        (2 * i + core, 2 * (i ^ orders[core][j]) + core)
        for i in range(count)
        for core in range(2)
    ]
    return lax.ppermute(value, ("seq", "dp"), pairs)


def widen(value, got):
    return jnp.concatenate([value, got], axis=0)


def give(total, orders, j):
    return hop(total[total.shape[0] // 2 :].astype(BF), orders, j)


def fold_all(keep, got):
    return keep + got.astype(F32)


def fold(total, got):
    return total[: total.shape[0] // 2] + got.astype(F32)


def halo(first, last):
    count = lax.axis_size("seq")
    low = lax.ppermute(last, "seq", [(i, i + 2) for i in range(count - 2)])
    high = lax.ppermute(first, "seq", [(i + 2, i) for i in range(count - 2)])
    return low, high


def swap_pair(value):
    count = lax.axis_size("seq")
    return lax.ppermute(value, "seq", [(i, i ^ 1) for i in range(count)])


def ordered(leading, mine, theirs):
    return jnp.concatenate(
        [jnp.where(leading, mine, theirs), jnp.where(leading, theirs, mine)], axis=0
    )


def split_pair(field, axis):
    even = lax.axis_index("seq") % 2 == 0
    half = field.shape[axis] // 2
    low = lax.slice_in_dim(field, 0, half, axis=axis)
    high = lax.slice_in_dim(field, half, 2 * half, axis=axis)
    return jnp.where(even, low, high), jnp.where(even, high, low)


def join_pair(mine, theirs, axis):
    even = lax.axis_index("seq") % 2 == 0
    return jnp.concatenate(
        [jnp.where(even, mine, theirs), jnp.where(even, theirs, mine)], axis=axis
    )


def with_weights(pieces, orders, middle, run):
    here, core = lax.axis_index("seq"), lax.axis_index("dp")
    own, other = pieces
    count, rows = own.shape[:2]
    part = rows // 4

    def case(taps, rest):
        def whole(ref, steps, half):
            cols = slice(half * middle, (half + 1) * middle)
            return jnp.concatenate(
                [ref[place_of(here ^ chip, steps), :, cols] for chip in range(count)], axis=0
            )

        def mix(h):
            pieces = []
            for chip in range(count):
                place = place_of(here ^ chip, orders[1])
                for lane in range(2):
                    start = (2 * lane + h) * part
                    pieces.append(rest[place, start : start + part, middle:])
            return jnp.concatenate(pieces, axis=0)

        run(
            [
                lambda: whole(taps, orders[0], 0),
                lambda: whole(taps, orders[0], 1),
                lambda: whole(rest, orders[1], 0),
            ],
            [lambda: mix(0), lambda: mix(1)],
        )

    @pl.when(core == 0)
    def _():
        case(own, other)

    @pl.when(core == 1)
    def _():
        case(other, own)


def norm_rows(source, w, start, size, target, put):
    @pl.loop(0, size // 32, unroll=4)
    def _(i):
        rows = pl.multiple_of(i * 32, 32)
        v = source[w, pl.ds(start + rows, 32), :].astype(F32)
        target[w, pl.ds(put + rows, 32), :] = gelu(v * norm_scale(v)).astype(BF)


def norm_kernel(x_ref, low_ref, high_ref, ext_ref):
    dilate = low_ref.shape[1]
    length = x_ref.shape[1]
    for w in range(x_ref.shape[0]):
        norm_rows(low_ref, w, 0, dilate, ext_ref, 0)
        norm_rows(x_ref, w, 0, length, ext_ref, dilate)
        norm_rows(high_ref, w, 0, dilate, ext_ref, dilate + length)


def norm_ext(x, low, high):
    windows, length, width = x.shape
    return pl.pallas_call(
        norm_kernel,
        out_shape=jax.ShapeDtypeStruct((windows, length + 2 * low.shape[1], width), BF),
        in_specs=[VMEM] * 3,
        out_specs=VMEM,
        compiler_params=params(),
        name="norm_ext",
    )(x, low, high)


def forward_kernel(
    orders, dilate, edge, ext, x_ref, own, other, pre_ref, hid_ref, x2_ref, first_ref, last_ref
):
    pieces = (own, other)
    windows, length, width = x_ref.shape
    middle = hid_ref.shape[1]

    def run(conv, mix):
        for w in range(windows):
            rows = slice(w * length, (w + 1) * length)
            pre = sum(dot(ext[w, k * dilate : k * dilate + length, :], conv[k]()) for k in range(3))
            pre_ref[rows, :] = pre
            hid = gelu(pre).astype(BF)
            hid_ref[rows, :] = hid
            for h in range(2):
                cols = slice(h * middle, (h + 1) * middle)
                x2_ref[w, :, cols] = (x_ref[w, :, cols].astype(F32) + dot(hid, mix[h]())).astype(BF)

    with_weights(pieces, orders, middle, run)
    for w in range(windows):
        norm_rows(x2_ref, w, 0, edge, first_ref, 0)
        norm_rows(x2_ref, w, length - edge, edge, last_ref, 0)


def forward_block(ext, x, pieces, orders, dilate, edge):
    windows, length, width = x.shape
    middle = pieces[0].shape[2] // 2
    flat = windows * length
    return pl.pallas_call(
        functools.partial(forward_kernel, orders, dilate, edge),
        out_shape=(
            jax.ShapeDtypeStruct((flat, middle), F32),
            jax.ShapeDtypeStruct((flat, middle), BF),
            jax.ShapeDtypeStruct(x.shape, BF),
            jax.ShapeDtypeStruct((windows, edge, width), BF),
            jax.ShapeDtypeStruct((windows, edge, width), BF),
        ),
        in_specs=[VMEM] * 4,
        out_specs=(VMEM,) * 5,
        compiler_params=params(),
        cost_estimate=cost(flat, width, middle),
        name="forward_block",
    )(ext, x, *pieces)


def turn_kernel(
    orders, dilate, first, last, low, high, x_ref, e_ref, own, other,
    ext, hid_ref, dpre_ref, dfirst, dlast,
):
    pieces = (own, other)
    windows, length, width = e_ref.shape
    edge = first.shape[1]
    middle = hid_ref.shape[1]
    for w in range(windows):
        for source, start in (
            (low, 0), (first, dilate), (last, dilate + length - edge), (high, dilate + length),
        ):
            ext[w, start : start + edge, :] = source[w]
        norm_rows(x_ref, w, edge, length - 2 * edge, ext, dilate + edge)

    def run(conv, mix):
        for w in range(windows):
            rows = slice(w * length, (w + 1) * length)
            pre = sum(dot(ext[w, k * dilate : k * dilate + length, :], conv[k]()) for k in range(3))
            dhid = dot(e_ref[w, :, :middle], mix[0](), NT) + dot(e_ref[w, :, middle:], mix[1](), NT)
            hid_ref[rows, :] = gelu(pre).astype(BF)
            dpre_ref[rows, :] = (gelu_slope(pre) * dhid).astype(BF)

    with_weights(pieces, orders, middle, run)
    for w in range(windows):
        dfirst[w] = dpre_ref[w * length : w * length + dilate, :]
        dlast[w] = dpre_ref[(w + 1) * length - dilate : (w + 1) * length, :]


def turn_block(first, last, low, high, x, e, pieces, orders, dilate):
    windows, length, width = e.shape
    middle = pieces[0].shape[2] // 2
    flat = windows * length
    return pl.pallas_call(
        functools.partial(turn_kernel, orders, dilate),
        out_shape=(
            jax.ShapeDtypeStruct((windows, length + 2 * dilate, width), BF),
            jax.ShapeDtypeStruct((flat, middle), BF),
            jax.ShapeDtypeStruct((flat, middle), BF),
            jax.ShapeDtypeStruct((windows, dilate, middle), BF),
            jax.ShapeDtypeStruct((windows, dilate, middle), BF),
        ),
        in_specs=[VMEM] * 8,
        out_specs=(VMEM,) * 5,
        compiler_params=params(),
        cost_estimate=cost(flat, width, middle),
        name="turn_block",
    )(first, last, low, high, x, e, *pieces)


def grads_kernel(orders, dilate, ext, hid, e_ref, dpre, keep, send, full):
    here, core = lax.axis_index("seq"), lax.axis_index("dp")
    windows, length, width = e_ref.shape
    middle = hid.shape[1]
    count, rows = keep.shape[:2]
    part = rows // 4

    def put(target, k):
        steps = orders[k // 2]
        cols = slice((k % 2) * middle, (k % 2 + 1) * middle)
        for chip in range(count):
            place = place_of(here ^ chip, steps)
            if k < 3:
                value = full[chip * rows : (chip + 1) * rows, :]
                target[place, :, cols] = value.astype(target.dtype)
                continue
            for lane in range(2):
                for h in range(2):
                    base = h * middle + (2 * chip + lane) * part
                    start = (2 * lane + h) * part
                    value = full[base : base + part, :]
                    target[place, start : start + part, cols] = value.astype(target.dtype)

    for k in range(4):
        if k == 3:
            for h in range(2):
                e = jnp.concatenate(
                    [e_ref[w, :, h * middle : (h + 1) * middle] for w in range(windows)], axis=0
                )
                full[h * middle : (h + 1) * middle, :] = dot(hid[...], e, TN)
        else:
            view = jnp.concatenate(
                [ext[w, k * dilate : k * dilate + length, :] for w in range(windows)], axis=0
            )
            full[...] = dot(view, dpre[...], TN)

        @pl.when(core == k // 2)
        def _():
            put(keep, k)

        @pl.when(core != k // 2)
        def _():
            put(send, k)


def grads_block(ext, hid, e, dpre, orders, dilate, count):
    windows, length, width = e.shape
    flat, middle = hid.shape
    shape = (count, width // count, 2 * middle)
    return pl.pallas_call(
        functools.partial(grads_kernel, orders, dilate),
        out_shape=(jax.ShapeDtypeStruct(shape, F32), jax.ShapeDtypeStruct(shape, BF)),
        in_specs=[VMEM] * 4,
        out_specs=(VMEM,) * 2,
        scratch_shapes=[pltpu.VMEM((width, middle), F32)],
        compiler_params=params(),
        cost_estimate=cost(flat, width, middle),
        name="grads_block",
    )(ext, hid, e, dpre)


def back_kernel(orders, dilate, orders_m, *refs):
    chained = orders_m is not None
    dpre, low, high, x_ref, e_ref = refs[:5]
    pieces = refs[5:7]
    if chained:
        pieces_m = refs[7:9]
        pre_ref, out_ref, dprev, dfirst, dlast, ext, dn = refs[9:]
    else:
        out_ref, ext, dn = refs[7:]
    windows, length, width = x_ref.shape
    middle = dpre.shape[1]
    for w in range(windows):
        ext[w, :dilate, :] = low[w]
        ext[w, dilate : dilate + length, :] = dpre[w * length : (w + 1) * length, :]
        ext[w, dilate + length :, :] = high[w]

    def run(conv, mix):
        for w in range(windows):
            dn[w] = sum(
                dot(ext[w, (2 - k) * dilate : (2 - k) * dilate + length, :], conv[k](), NT)
                for k in range(3)
            )

    with_weights(pieces, orders, middle, run)
    for w in range(windows):

        @pl.loop(0, length // 32, unroll=4)
        def _(i):
            rows = pl.ds(pl.multiple_of(i * 32, 32), 32)
            v = x_ref[w, rows, :].astype(F32)
            scale = norm_scale(v)
            u = v * scale
            g = dn[w, rows, :] * gelu_slope(u)
            dv = scale * (g - u * jnp.mean(g * u, axis=-1, keepdims=True))
            out_ref[w, rows, :] = (e_ref[w, rows, :].astype(F32) + dv).astype(BF)

    if chained:

        def turn(conv, mix):
            for w in range(windows):
                dhid = dot(out_ref[w, :, :middle], mix[0](), NT) + dot(
                    out_ref[w, :, middle:], mix[1](), NT
                )
                rows = slice(w * length, (w + 1) * length)
                dprev[rows, :] = (gelu_slope(pre_ref[rows, :]) * dhid).astype(BF)

        with_weights(pieces_m, orders_m, middle, turn)
        edge = dfirst.shape[1]
        for w in range(windows):
            dfirst[w] = dprev[w * length : w * length + edge, :]
            dlast[w] = dprev[(w + 1) * length - edge : (w + 1) * length, :]


def back_block(dpre, low, high, x, e, pieces, orders, dilate, previous=None):
    windows, length, width = x.shape
    flat, middle = dpre.shape
    chained, orders_m = previous is not None, None
    operands = [dpre, low, high, x, e, *pieces]
    shapes = [jax.ShapeDtypeStruct(x.shape, BF)]
    if chained:
        others, orders_m, pre, edge = previous
        operands += [*others, pre]
        shapes += [
            jax.ShapeDtypeStruct((flat, middle), BF),
            jax.ShapeDtypeStruct((windows, edge, middle), BF),
            jax.ShapeDtypeStruct((windows, edge, middle), BF),
        ]
    return pl.pallas_call(
        functools.partial(back_kernel, orders, dilate, orders_m),
        out_shape=tuple(shapes),
        in_specs=[VMEM] * len(operands),
        out_specs=(VMEM,) * len(shapes),
        scratch_shapes=[
            pltpu.VMEM((windows, length + 2 * dilate, middle), BF),
            pltpu.VMEM((windows, length, width), F32),
        ],
        compiler_params=params(),
        cost_estimate=cost(flat, width, middle),
        name="back_block",
    )(*operands)


def pack(conv, mix):
    middle = conv.shape[2]
    first = conv[:, :2].reshape(conv.shape[0], 2 * middle)
    tall = jnp.concatenate([mix[:, :middle], mix[:, middle:]], axis=0)
    second = jnp.concatenate([conv[:, 2], tall], axis=1)
    return first, second


def unpack(total, middle):
    rows = total.shape[0] // 2
    leading = lax.axis_index("dp") == 0
    got = cross(jnp.where(leading, total[rows:], total[:rows]))
    first = jnp.where(leading, total[:rows], got)
    second = jnp.where(leading, got, total[rows:])
    conv = jnp.concatenate(
        [first.reshape(rows, 2, middle), second[:, None, :middle]], axis=1
    )
    half = rows // 2
    mix = jnp.concatenate([second[:half, middle:], second[half:, middle:]], axis=1)
    return conv, mix


def body(activations, cotangent, conv_one, mix_one, conv_two, mix_two):
    count = lax.axis_size("seq")
    orders = step_orders(count, GATHER_ONE)
    orders_two = step_orders(count, GATHER_TWO)
    sums_one = step_orders(count, SUM_ONE)
    sums_two = step_orders(count, SUM_TWO)
    last_step = len(orders[0]) - 1
    middle = conv_one.shape[2]
    leading = lax.axis_index("dp") == 0

    def chip_part(conv, mix):
        first, second = pack(conv, mix)
        got = cross(jnp.where(leading, second, first))
        return ordered(leading, jnp.where(leading, first, second), got)[None]

    mine_x, gives_x = split_pair(activations, 0)
    got_x = swap_pair(gives_x)
    own_one = chip_part(conv_one, mix_one)
    got_one = hop(own_one, orders, 0)
    conv_two, mix_two, own_one = tie(conv_two, mix_two, own_one)
    own_two = chip_part(conv_two, mix_two)
    own_one = widen(own_one, got_one)
    got_one = hop(own_one, orders, 1)
    got_two = hop(own_two, orders_two, 0)
    own_one, cotangent, got_x = tie(own_one, cotangent, got_x)
    x = join_pair(mine_x, got_x, 1)
    length = x.shape[1]
    low, high = halo(x[:, :DILATE_ONE], x[:, length - DILATE_ONE :])
    mine_e, gives_e = split_pair(cotangent, 0)
    got_e = swap_pair(gives_e)
    ext_one = norm_ext(x, low, high)
    got_one, got_two, ext_one, got_e = tie(got_one, got_two, ext_one, got_e)
    for j in range(2, last_step + 1):
        own_one, own_two = widen(own_one, got_one), widen(own_two, got_two)
        got_one, got_two = hop(own_one, orders, j), hop(own_two, orders_two, j - 1)
        if j == last_step:
            e = join_pair(mine_e, got_e, 1)
        got_one, got_two = tie(got_one, got_two)
    own_one = widen(own_one, got_one)
    got_one = cross(own_one)
    own_one, got_two = tie(own_one, got_two)
    own_two = widen(own_two, got_two)
    got_two = hop(own_two, orders_two, last_step)
    pieces_one = (own_one, got_one)
    pre_one, hid_one, second_in, first, last = forward_block(
        ext_one, x, pieces_one, orders, DILATE_ONE, DILATE_TWO
    )
    low, high = halo(first, last)
    got_two, low, high = tie(got_two, low, high)
    own_two = widen(own_two, got_two)
    pieces_two = (own_two, cross(own_two))
    ext_two, hid_two, dpre_two, dfirst, dlast = turn_block(
        first, last, low, high, second_in, e, pieces_two, orders_two, DILATE_TWO
    )

    dlow, dhigh = halo(dfirst, dlast)
    keep_two, send = grads_block(
        ext_two, hid_two, e, dpre_two, sums_two, DILATE_TWO, count
    )
    dlow, dhigh, send = tie(dlow, dhigh, send)
    got_two = cross(send)
    upstream, dpre_one, dfirst, dlast = back_block(
        dpre_two, dlow, dhigh, second_in, e, pieces_two, orders_two, DILATE_TWO,
        (pieces_one, orders, pre_one, DILATE_ONE),
    )
    got_two, dpre_one, upstream = tie(got_two, dpre_one, upstream)
    total_two = fold_all(keep_two, got_two)
    total_two, dpre_one = tie(total_two, dpre_one)
    got_two = give(total_two, sums_two, last_step)
    keep_one, send = grads_block(ext_one, hid_one, upstream, dpre_one, sums_one, DILATE_ONE, count)
    got_one = cross(send)
    dfirst, dlast, send = tie(dfirst, dlast, send)
    dlow, dhigh = halo(dfirst, dlast)
    total_one = fold_all(keep_one, got_one)
    got_two, total_one, dlow, dhigh = tie(got_two, total_one, dlow, dhigh)
    got_one = give(total_one, sums_one, last_step)
    total_two = fold(total_two, got_two)
    got_two = give(total_two, sums_two, last_step - 1)
    (input_grad,) = back_block(
        dpre_one, dlow, dhigh, x, upstream, pieces_one, orders, DILATE_ONE
    )
    input_grad, got_one, got_two = tie(input_grad, got_one, got_two)
    mine_g, gives_g = split_pair(input_grad, 1)
    for j in reversed(range(last_step)):
        if j < last_step - 1:
            total_two = fold(total_two, got_two)
            got_two = give(total_two, sums_two, j)
        total_one = fold(total_one, got_one)
        got_one = give(total_one, sums_one, j)
        if j == last_step - 1:
            got_one, gives_g = tie(got_one, gives_g)
            got_g = swap_pair(gives_g)
    total_two = fold(total_two, got_two)
    grads_two = unpack(total_two[0], middle)
    got_one, got_g = tie(got_one, got_g)
    total_one = fold(total_one, got_one)
    input_grad = join_pair(mine_g, got_g, 0)
    return (input_grad, *unpack(total_one[0], middle), *grads_two)


def solution(mesh):
    in_specs = (
        P(("parts", "dp"), "seq", None),
        P(("parts", "dp"), "seq", None),
        P(("seq", "dp"), None, None),
        P(("seq", "dp"), None),
        P(("seq", "dp"), None, None),
        P(("seq", "dp"), None),
    )
    out_specs = (
        P(("parts", "dp"), "seq", None),
        P(("parts", "seq", "dp"), None, None),
        P(("parts", "seq", "dp"), None),
        P(("parts", "seq", "dp"), None, None),
        P(("parts", "seq", "dp"), None),
    )
    return jax.shard_map(body, mesh=mesh, in_specs=in_specs, out_specs=out_specs, check_vma=False)
```
